128 devices in a mesh: section: 4 (over x), tensor: 32 (over y, z, core).
Axes of the slice: x: 4, y: 4, z: 4, core: 2. Of those that a mesh axis runs over, the one named last changes fastest.
Arguments:
- hidden_last: bfloat16 [512, 6656], P(None, 'tensor'), may hold values from -6 to 6
- labels: int32 [512], replicated, may hold values from 0 to 31999
- head_weight: bfloat16 [6656, 32000], P(None, 'tensor'), may hold values from -0.21875 to 0.21875
- layer_inputs: bfloat16 [4, 512, 6656], P('section', None, 'tensor'), may hold values from -6 to 6
- weights: bfloat16 [4, 6656, 6656], P('section', 'tensor'), may hold values from -0.078125 to 0.078125
- row_state: float32 [4, 6656], P('section', 'tensor'), may hold values from 1.173753e-06 to 0.000498845
- col_state: float32 [4, 6656], P('section'), may hold values from 1e-08 to 1e-06
Outputs:
- loss: float32 [], replicated
- input_grads: bfloat16 [4, 512, 6656], P('section', None, 'tensor')
- new_weights: bfloat16 [4, 6656, 6656], P('section', 'tensor')
- new_row_state: float32 [4, 6656], P('section', 'tensor')
- new_col_state: float32 [4, 6656], P('section')
The draws below stay inside these ranges and needn't reach their ends.
All inputs are finite; a program needn't handle non-finite values.
Results may differ from the reference program's by a relative error of at most 0.007.
Values may be sent and summed in bfloat16 or wider, within the bound.
No kernel may reach another device: no remote copies, remote signals or barrier semaphores. Data moves between devices by JAX's collectives and lax.ppermute only.
A program may use at most 128 MiB of HBM per device.

```python
import math
import jax
import jax.numpy as jnp
from jax import lax

D = 6656
VOCAB = 32000
SECTIONS = 4
TOKENS = 512


def draw_row_state(key, part):
    base_scale = 9.0 / (TOKENS * D)
    end_factor = 30.0
    position = jnp.arange(D, dtype=jnp.float32) / (D - 1)
    rising = jnp.exp(position * math.log(end_factor))
    roughness = jnp.exp(jax.random.uniform(key, (SECTIONS, D), jnp.float32, math.log(0.5), math.log(2.0)))
    return (base_scale * rising[None, :] * roughness).astype(jnp.float32)


def with_ends(result, key, least, largest):
    longest = result.shape.index(max(result.shape))
    spots = []
    for shift in (0, 1):
        where = [jax.random.randint(jax.random.fold_in(key, axis), (), 0, length) for axis, length in enumerate(result.shape)]
        where[longest] = (where[longest] + shift) % result.shape[longest]
        spots.append(tuple(where))
    return result.at[spots[0]].set(least).at[spots[1]].set(largest)


def block_levels(stream_key, shape, cuts, smallest, high):
    factor_of, own = 1.0, jax.random.fold_in(stream_key, 6)
    for dim, shards_of in cuts:
        draws = jnp.exp(jax.random.uniform(jax.random.fold_in(own, dim), (shards_of,), jnp.float32, smallest / len(cuts), high / len(cuts)))
        factor_of = factor_of * jnp.repeat(draws, shape[dim] // shards_of).reshape([-1 if axis == dim else 1 for axis in range(len(shape))])
    return factor_of


def scatter_about(stream_key, dims, deviation, limit, shards=(), kind=jnp.bfloat16):
    gain = block_levels(stream_key, dims, shards, -0.22, 0.18) if shards else 1.0
    drawn = jax.random.normal(stream_key, dims, jnp.float32) * deviation * gain
    return jnp.minimum(jnp.maximum(drawn, -limit), limit).astype(kind)


def setup_inputs(seed: int = 0) -> dict:
    key_of = jax.random.split(jax.random.key(seed), 8)
    return {
        "hidden_last": scatter_about(key_of[0], (TOKENS, D), 1.0, 6.0, ((1, 32),)),
        "labels": with_ends(jax.random.randint(key_of[1], (TOKENS,), 0, VOCAB), jax.random.fold_in(key_of[1], 1), 0, VOCAB - 1).astype(jnp.int32),
        "head_weight": scatter_about(key_of[2], (D, VOCAB), (D // 9) ** -0.5, 0.21875, ((1, 32),)),
        "layer_inputs": scatter_about(key_of[3], (SECTIONS, TOKENS, D), 1.0, 6.0, ((0, 4), (2, 32))),
        "weights": scatter_about(key_of[4], (SECTIONS, D, D), D ** -0.5, 0.078125, ((0, 4), (1, 32))),
        "row_state": draw_row_state(jax.random.fold_in(key_of[7], 71), 0),
        "col_state": jnp.clip(jnp.exp(math.log(9.999999974752427e-07) - 4.6051702 * jax.random.uniform(key_of[6], (SECTIONS, D), jnp.float32) ** block_levels(key_of[6], (SECTIONS, D), ((0, 4),), -0.2, 0.2)), 9.99999993922529e-09, 9.999999974752427e-07),
    }


decay_rate = 0.9
learn_rate = 0.3
tiny_term = 1e-30

def adalomo(gradient, weight, row_prev, col_prev):
    model_width = weight.shape[0]
    squares = gradient * gradient + tiny_term
    row_new = decay_rate * row_prev + (1.0 - decay_rate) * lax.optimization_barrier(jnp.mean(squares, axis=1))
    col_new = decay_rate * col_prev + (1.0 - decay_rate) * lax.optimization_barrier(jnp.mean(squares, axis=0))
    second = row_new[:, None] * col_new[None, :] / jnp.sum(row_new)
    update = gradient / jnp.sqrt(second)
    entries = float(model_width * model_width)
    weight_float = weight.astype(jnp.float32)
    update_rms = jnp.sqrt(jnp.sum(update * update) / entries)
    weight_rms = jnp.sqrt(jnp.sum(weight_float * weight_float) / entries)
    factor = learn_rate * weight_rms / jnp.maximum(1.0, update_rms)
    return ((weight_float - factor * update).astype(jnp.bfloat16), row_new, col_new)

def reference(hidden_last, labels, head_weight, layer_inputs, weights, row_state, col_state):
    all_rows = labels.shape[0]
    logits = jnp.dot(hidden_last, head_weight, preferred_element_type=jnp.float32)
    exponent = jnp.exp(logits)
    label_hit = labels[:, None] == jnp.arange(head_weight.shape[1], dtype=jnp.int32)[None, :]
    denominator = lax.optimization_barrier(jnp.sum(exponent, axis=1))
    picked = lax.optimization_barrier(jnp.sum(jnp.where(label_hit, logits, jnp.zeros_like(logits)), axis=1))
    loss = jnp.sum(jnp.log(denominator) - picked) / all_rows
    logit_grad = ((exponent / denominator[:, None] - label_hit.astype(jnp.float32)) / all_rows).astype(jnp.bfloat16)
    carried = jnp.dot(logit_grad, head_weight.T, preferred_element_type=jnp.float32).astype(jnp.bfloat16)
    grads_list, weight_list, row_list, col_list = ([], [], [], [])
    for layer_index in reversed(range(weights.shape[0])):
        weight = weights[layer_index]
        saved = layer_inputs[layer_index]
        backward = jnp.dot(carried, weight.T, preferred_element_type=jnp.float32)
        input_grad = (carried.astype(jnp.float32) + backward).astype(jnp.bfloat16)
        gradient = jnp.dot(saved.T, carried, preferred_element_type=jnp.float32)
        new_weight, row_new, col_new = adalomo(gradient, weight, row_state[layer_index], col_state[layer_index])
        grads_list.insert(0, input_grad)
        weight_list.insert(0, new_weight)
        row_list.insert(0, row_new)
        col_list.insert(0, col_new)
        carried = input_grad
    return (loss, jnp.stack(grads_list), jnp.stack(weight_list), jnp.stack(row_list), jnp.stack(col_list))
```

```python
import jax
import jax.numpy as jnp
from jax import lax
from jax.sharding import Mesh, PartitionSpec as P

decay_rate = 0.9
learn_rate = 0.3
tiny_term = 1e-30
bf16_largest = 3.3895e38


def from_ring(block, axis):
    size = lax.axis_size(axis)
    return [block] + [
        lax.ppermute(block, axis, [(i, (i - step) % size) for i in range(size)])
        for step in range(1, size)
    ]


def rotated(pieces, index, axis=0):
    count = len(pieces)
    placed = []
    for k in range(count):
        chosen = pieces[k]
        for shift in range(1, count):
            chosen = jnp.where(index == shift, pieces[(k - shift) % count], chosen)
        placed.append(chosen)
    return jnp.stack(placed, axis=axis)


def gathered(block, axis, at=0):
    return rotated(from_ring(block, axis), lax.axis_index(axis), at)


def gathered_tensor(block):
    return gathered(gathered(gathered(block, "z"), "y"), "c", 2).reshape(-1, block.shape[-1])


def summed(x, axis):
    pieces = from_ring(x, axis)
    if len(pieces) == 2:
        return pieces[0] + pieces[1]
    return (pieces[0] + pieces[2]) + (pieces[1] + pieces[3])


def summed_tensor(x):
    return summed(summed(summed(x, "c"), "z"), "y")


def scattered(blocks, axis):
    size = lax.axis_size(axis)
    index = lax.axis_index(axis)
    total = None
    for step in range(size):
        piece = blocks[step]
        for shift in range(1, size):
            piece = jnp.where(index == shift, blocks[(step + shift) % size], piece)
        if step:
            piece = lax.ppermute(
                piece.astype(jnp.bfloat16), axis, [(i, (i + step) % size) for i in range(size)]
            )
        piece = piece.astype(jnp.float32)
        total = piece if total is None else total + piece
    return total


def body(hidden_last, labels, head_weight, layer_inputs, weights, row_state, col_state):
    section_count = lax.axis_size("x")
    section_index = lax.axis_index("x")
    core = lax.axis_index("c")
    all_rows = labels.shape[0]
    model_width, vocab_local = head_weight.shape
    local_weight = weights[0]
    rows_local = local_weight.shape[0]
    saved_all = layer_inputs[0]
    tensor_index = lax.axis_index(("y", "z", "c"))
    columns = tensor_index * vocab_local + lax.iota(jnp.int32, vocab_local)
    share = all_rows // section_count
    row_start = section_index * share
    entries = float(model_width * model_width)

    hidden_rows = lax.dynamic_slice_in_dim(hidden_last, row_start, share, 0).T
    hidden_all = gathered_tensor(hidden_rows)
    logits = lax.dot_general(
        head_weight, hidden_all, (((0,), (0,)), ((), ())), preferred_element_type=jnp.float32
    )
    exponent = jnp.exp(logits)
    label_hit = lax.dynamic_slice_in_dim(labels, row_start, share, 0)[None, :] == columns[:, None]
    weight_float = local_weight.astype(jnp.float32)
    weight_part = jnp.broadcast_to(jnp.sum(weight_float * weight_float), (share,))
    sums = summed_tensor(
        jnp.stack(
            [
                jnp.sum(exponent, axis=0),
                jnp.sum(jnp.where(label_hit, logits, jnp.zeros_like(logits)), axis=0),
                weight_part,
            ]
        )
    )
    denominator, picked, weight_total = sums[0], sums[1], sums[2, 0]
    both = jnp.concatenate(
        [jnp.minimum(exponent, bf16_largest).astype(jnp.bfloat16), label_hit.astype(jnp.bfloat16)], axis=1
    )
    product = jnp.dot(head_weight, both, preferred_element_type=jnp.float32)
    part = (product[:, :share] / denominator[None, :] - product[:, share:]) / all_rows
    part = part.reshape(4, 4, 2, rows_local, share)
    part = scattered([part[:, :, 0], part[:, :, 1]], "c")
    part = scattered(part, "y")
    part = scattered(part, "z")
    head_grad = gathered(part.astype(jnp.bfloat16), "x", 1).reshape(rows_local, all_rows)
    loss = summed(jnp.sum(jnp.log(denominator) - picked)[None], "x")[0] / all_rows

    dy = head_grad
    outputs = jnp.zeros((rows_local, all_rows), jnp.bfloat16)
    gradient = jnp.zeros((rows_local, model_width), jnp.float32)
    for step in range(4):
        active = step == section_count - 1 - section_index
        full = lax.all_gather(dy, ("y", "z", "c"), axis=0, tiled=True)
        backward = jnp.dot(local_weight, full, preferred_element_type=jnp.float32)
        input_grad = (dy.astype(jnp.float32) + backward).astype(jnp.bfloat16)
        outputs = jnp.where(active, input_grad, outputs)
        if step < 3:
            dy = lax.ppermute(input_grad, "x", [(i, i - 1) for i in range(1, 4)])
        gradient = lax.cond(
            active,
            lambda g, f: lax.dot_general(
                saved_all, f, (((0,), (1,)), ((), ())), preferred_element_type=jnp.float32
            ),
            lambda g, f: g,
            gradient,
            full,
        )

    squares = gradient * gradient
    row_new = decay_rate * row_state[0] + (1.0 - decay_rate) * jnp.mean(squares + tiny_term, axis=1)
    col_part = jnp.sum(squares + tiny_term, axis=0)
    scaled_part = jnp.sum(squares * (1.0 / row_new)[:, None], axis=0)
    row_part = jnp.broadcast_to(jnp.sum(row_new), (128,))
    payload = jnp.concatenate([col_part, scaled_part, row_part]).reshape(-1, 128)
    payload = summed_tensor(payload).reshape(-1)
    col_sum = payload[:model_width]
    scaled_sum = payload[model_width : 2 * model_width]
    row_total = payload[2 * model_width]
    col_new = decay_rate * col_state[0] + (1.0 - decay_rate) * (col_sum / model_width)
    update_total = row_total * jnp.sum(scaled_sum / col_new)
    factor = (
        learn_rate
        * jnp.sqrt(weight_total / entries)
        / jnp.maximum(1.0, jnp.sqrt(update_total / entries))
    )
    row_scale = factor * jnp.sqrt(row_total / row_new)
    col_scale = 1.0 / jnp.sqrt(col_new)
    new_weight = (weight_float - gradient * row_scale[:, None] * col_scale[None, :]).astype(jnp.bfloat16)
    return (loss, outputs.T[None], new_weight[None], row_new[None], col_new[None])


def solution(mesh):
    fine = Mesh(mesh.devices.reshape(4, 4, 4, 2), ("x", "y", "z", "c"))
    tensor = ("y", "z", "c")
    return jax.shard_map(
        body,
        mesh=fine,
        in_specs=(
            P(None, tensor),
            P(),
            P(None, tensor),
            P("x", None, tensor),
            P("x", tensor, None),
            P("x", tensor),
            P("x", None),
        ),
        out_specs=(
            P(),
            P("x", None, tensor),
            P("x", tensor, None),
            P("x", tensor),
            P("x", None),
        ),
        check_vma=False,
    )
```

```python
import jax
import jax.numpy as jnp
from jax import lax
from jax.sharding import Mesh, PartitionSpec as P

decay_rate = 0.9
learn_rate = 0.3
tiny_term = 1e-30
bf16_largest = 3.3895e38


def from_ring(block, axis):
    size = lax.axis_size(axis)
    return [block] + [
        lax.ppermute(block, axis, [(i, (i - step) % size) for i in range(size)])
        for step in range(1, size)
    ]


def rotated(pieces, index, axis=0):
    count = len(pieces)
    placed = []
    for k in range(count):
        chosen = pieces[k]
        for shift in range(1, count):
            chosen = jnp.where(index == shift, pieces[(k - shift) % count], chosen)
        placed.append(chosen)
    return jnp.stack(placed, axis=axis)


def gathered(block, axis, at=0):
    return rotated(from_ring(block, axis), lax.axis_index(axis), at)


def gathered_tensor(block):
    return gathered(gathered(gathered(block, "z"), "y"), "c", 2).reshape(-1, block.shape[-1])


def summed(x, axis):
    pieces = from_ring(x, axis)
    if len(pieces) == 2:
        return pieces[0] + pieces[1]
    return (pieces[0] + pieces[2]) + (pieces[1] + pieces[3])


def summed_tensor(x):
    return summed(summed(summed(x, "c"), "z"), "y")


def scattered(blocks, axis):
    size = lax.axis_size(axis)
    index = lax.axis_index(axis)
    total = None
    for step in range(size):
        piece = blocks[step]
        for shift in range(1, size):
            piece = jnp.where(index == shift, blocks[(step + shift) % size], piece)
        if step:
            piece = lax.ppermute(
                piece.astype(jnp.bfloat16), axis, [(i, (i + step) % size) for i in range(size)]
            )
        piece = piece.astype(jnp.float32)
        total = piece if total is None else total + piece
    return total


def exchanged(blocks, axis):
    size = lax.axis_size(axis)
    index = lax.axis_index(axis)
    pieces = []
    for step in range(size):
        piece = blocks[step]
        for shift in range(1, size):
            piece = jnp.where(index == shift, blocks[(step + shift) % size], piece)
        if step:
            piece = lax.ppermute(piece, axis, [(i, (i + step) % size) for i in range(size)])
        pieces.append(piece)
    return rotated([pieces[-k % size] for k in range(size)], index, 1)


def body(hidden_last, labels, head_weight, layer_inputs, weights, row_state, col_state):
    section_count = lax.axis_size("x")
    section_index = lax.axis_index("x")
    core = lax.axis_index("c")
    all_rows = labels.shape[0]
    model_width, vocab_local = head_weight.shape
    local_weight = weights[0]
    rows_local = local_weight.shape[0]
    saved_all = layer_inputs[0]
    tensor_index = lax.axis_index(("y", "z", "c"))
    columns = tensor_index * vocab_local + lax.iota(jnp.int32, vocab_local)
    share = all_rows // section_count
    row_start = section_index * share
    entries = float(model_width * model_width)

    all_weights = lax.all_gather(local_weight, "x", axis=0)
    hidden_rows = lax.dynamic_slice_in_dim(hidden_last, row_start, share, 0).T
    hidden_all = gathered_tensor(hidden_rows)
    logits = lax.dot_general(
        head_weight, hidden_all, (((0,), (0,)), ((), ())), preferred_element_type=jnp.float32
    )
    exponent = jnp.exp(logits)
    label_hit = lax.dynamic_slice_in_dim(labels, row_start, share, 0)[None, :] == columns[:, None]
    weight_float = local_weight.astype(jnp.float32)
    weight_part = jnp.broadcast_to(jnp.sum(weight_float * weight_float), (share,))
    sums = summed_tensor(
        jnp.stack(
            [
                jnp.sum(exponent, axis=0),
                jnp.sum(jnp.where(label_hit, logits, jnp.zeros_like(logits)), axis=0),
                weight_part,
            ]
        )
    )
    denominator, picked, weight_total = sums[0], sums[1], sums[2, 0]
    both = jnp.concatenate(
        [jnp.minimum(exponent, bf16_largest).astype(jnp.bfloat16), label_hit.astype(jnp.bfloat16)], axis=1
    )
    product = jnp.dot(head_weight, both, preferred_element_type=jnp.float32)
    part = (product[:, :share] / denominator[None, :] - product[:, share:]) / all_rows
    part = part.reshape(4, 4, 2, rows_local, share)
    part = scattered([part[:, :, 0], part[:, :, 1]], "c")
    part = scattered(part, "y")
    part = scattered(part, "z")
    carried = part.astype(jnp.bfloat16)
    loss = summed(jnp.sum(jnp.log(denominator) - picked)[None], "x")[0] / all_rows

    chain = [carried]
    for layer in reversed(range(section_count)):
        full = gathered_tensor(carried)
        backward = jnp.dot(all_weights[layer], full, preferred_element_type=jnp.float32)
        carried = (carried.astype(jnp.float32) + backward).astype(jnp.bfloat16)
        chain.insert(0, carried)

    dy = exchanged(chain[1:], "x").reshape(rows_local, all_rows)
    outputs = exchanged(chain[:-1], "x").reshape(rows_local, all_rows)
    full = lax.all_gather(dy, ("y", "z", "c"), axis=0, tiled=True)
    gradient = lax.dot_general(
        saved_all, full, (((0,), (1,)), ((), ())), preferred_element_type=jnp.float32
    )

    squares = gradient * gradient
    row_new = decay_rate * row_state[0] + (1.0 - decay_rate) * jnp.mean(squares + tiny_term, axis=1)
    col_part = jnp.sum(squares + tiny_term, axis=0)
    scaled_part = jnp.sum(squares * (1.0 / row_new)[:, None], axis=0)
    row_part = jnp.broadcast_to(jnp.sum(row_new), (128,))
    payload = jnp.concatenate([col_part, scaled_part, row_part]).reshape(-1, 128)
    payload = summed_tensor(payload).reshape(-1)
    col_sum = payload[:model_width]
    scaled_sum = payload[model_width : 2 * model_width]
    row_total = payload[2 * model_width]
    col_new = decay_rate * col_state[0] + (1.0 - decay_rate) * (col_sum / model_width)
    update_total = row_total * jnp.sum(scaled_sum / col_new)
    factor = (
        learn_rate
        * jnp.sqrt(weight_total / entries)
        / jnp.maximum(1.0, jnp.sqrt(update_total / entries))
    )
    row_scale = factor * jnp.sqrt(row_total / row_new)
    col_scale = 1.0 / jnp.sqrt(col_new)
    new_weight = (weight_float - gradient * row_scale[:, None] * col_scale[None, :]).astype(jnp.bfloat16)
    return (loss, outputs.T[None], new_weight[None], row_new[None], col_new[None])


def solution(mesh):
    fine = Mesh(mesh.devices.reshape(4, 4, 4, 2), ("x", "y", "z", "c"))
    tensor = ("y", "z", "c")
    return jax.shard_map(
        body,
        mesh=fine,
        in_specs=(
            P(None, tensor),
            P(),
            P(None, tensor),
            P("x", None, tensor),
            P("x", tensor, None),
            P("x", tensor),
            P("x", None),
        ),
        out_specs=(
            P(),
            P("x", None, tensor),
            P("x", tensor, None),
            P("x", tensor),
            P("x", None),
        ),
        check_vma=False,
    )
```

```python
import jax
import jax.numpy as jnp
from jax import lax
from jax.experimental import pallas as pl
from jax.experimental.pallas import tpu as pltpu
from jax.sharding import Mesh, PartitionSpec as P

decay_rate = 0.9
learn_rate = 0.3
tiny_term = 1e-30
bf16_largest = 3.3895e38
wide_vmem = 48 * 1024 * 1024


def from_ring(block, axis):
    size = lax.axis_size(axis)
    return [block] + [
        lax.ppermute(block, axis, [(i, (i - step) % size) for i in range(size)])
        for step in range(1, size)
    ]


def rotated(pieces, index, axis=0):
    count = len(pieces)
    placed = []
    for k in range(count):
        chosen = pieces[k]
        for shift in range(1, count):
            chosen = jnp.where(index == shift, pieces[(k - shift) % count], chosen)
        placed.append(chosen)
    return jnp.stack(placed, axis=axis)


def tensor_pieces(block):
    mine = from_ring(jnp.stack(from_ring(block, "z")), "y")
    return mine + [lax.ppermute(piece, "c", [(0, 1), (1, 0)]) for piece in mine]


def summed(x, axis):
    pieces = from_ring(x, axis)
    if len(pieces) == 2:
        return pieces[0] + pieces[1]
    return (pieces[0] + pieces[2]) + (pieces[1] + pieces[3])


def summed_tensor(x):
    return summed(summed(summed(x, "c"), "z"), "y")


def scattered(blocks, axis):
    size = len(blocks)
    total = blocks[0].astype(jnp.float32)
    for step in range(1, size):
        piece = lax.ppermute(blocks[step], axis, [(i, (i + step) % size) for i in range(size)])
        total = total + piece.astype(jnp.float32)
    return total


def exchanged(blocks, axis):
    size = lax.axis_size(axis)
    index = lax.axis_index(axis)
    pieces = []
    for step in range(size):
        piece = blocks[step]
        for shift in range(1, size):
            piece = jnp.where(index == shift, blocks[(step + shift) % size], piece)
        if step:
            piece = lax.ppermute(piece, axis, [(i, (i + step) % size) for i in range(size)])
        pieces.append(piece)
    return rotated([pieces[-k % size] for k in range(size)], index, 1)


def place(pieces, place_ref, full_ref):
    y, z, c = place_ref[0], place_ref[1], place_ref[2]
    rows = pieces[0].shape[1]
    for side in range(2):
        for step_y in range(4):
            for step_z in range(4):
                chip = lax.rem(y + step_y, 4) * 4 + lax.rem(z + step_z, 4)
                core = c if side == 0 else 1 - c
                start = pl.multiple_of((chip * 2 + core) * rows, 16)
                full_ref[pl.ds(start, rows), :] = pieces[side * 4 + step_y][step_z]


def logits_kernel(place_ref, *refs):
    pieces, (labels_ref, weight_ref, both_ref, sums_ref, full_ref, total_ref) = refs[:8], refs[8:]
    step = pl.program_id(0)
    depth = weight_ref.shape[1]
    share = labels_ref.shape[1]

    @pl.when(step == 0)
    def _():
        place(pieces, place_ref, full_ref)
        total_ref[...] = jnp.zeros_like(total_ref)

    rows = full_ref[pl.ds(pl.multiple_of(step * depth, depth), depth), :]
    total_ref[...] += jnp.dot(weight_ref[...], rows, preferred_element_type=jnp.float32)

    @pl.when(step == pl.num_programs(0) - 1)
    def _():
        logits = total_ref[...]
        exponent = jnp.exp(logits)
        columns = place_ref[3] + lax.broadcasted_iota(jnp.int32, logits.shape, 0)
        label_hit = columns == labels_ref[...]
        sums_ref[0:1, :] = jnp.sum(exponent, axis=0, keepdims=True)
        sums_ref[1:2, :] = jnp.sum(jnp.where(label_hit, logits, 0.0), axis=0, keepdims=True)
        both_ref[:, :share] = jnp.minimum(exponent, bf16_largest).astype(jnp.bfloat16)
        both_ref[:, share:] = jnp.where(label_hit, 1.0, 0.0).astype(jnp.bfloat16)


def head_logits(where, pieces, labels, weight, tile=512):
    vocab_local, model_width = weight.shape
    share = labels.shape[1]
    whole = lambda shape: pl.BlockSpec(shape, lambda i, s: (0,) * len(shape))
    return pl.pallas_call(
        logits_kernel,
        grid_spec=pltpu.PrefetchScalarGridSpec(
            num_scalar_prefetch=1,
            grid=(model_width // tile,),
            in_specs=[whole(p.shape) for p in pieces]
            + [whole(labels.shape), pl.BlockSpec((vocab_local, tile), lambda i, s: (0, i))],
            out_specs=[whole((vocab_local, 2 * share)), whole((2, share))],
            scratch_shapes=[
                pltpu.VMEM((model_width, share), jnp.bfloat16),
                pltpu.VMEM((vocab_local, share), jnp.float32),
            ],
        ),
        out_shape=[
            jax.ShapeDtypeStruct((vocab_local, 2 * share), jnp.bfloat16),
            jax.ShapeDtypeStruct((2, share), jnp.float32),
        ],
        compiler_params=pltpu.CompilerParams(vmem_limit_bytes=wide_vmem),
    )(where, *pieces, labels, weight)


def combine_kernel(place_ref, product_ref, sums_ref, keep_ref, send_ref, turned_ref):
    share = sums_ref.shape[1]
    rows = keep_ref.shape[2]
    z, c = place_ref[1], place_ref[2]
    scale = (1.0 / place_ref[4].astype(jnp.float32)) / sums_ref[0:1, :]
    scale = jnp.broadcast_to(scale, (share, share)).T
    unit = 1.0 / place_ref[4].astype(jnp.float32)
    for at in range(0, product_ref.shape[1], share):
        block = product_ref[:share, at : at + share] * scale - product_ref[share:, at : at + share] * unit
        turned_ref[at : at + share, :] = block.T
    for step in range(4):
        chip = lax.rem(z + step, 4) * 2
        keep_ref[0, step] = turned_ref[pl.ds(pl.multiple_of((chip + c) * rows, 16), rows), :]
        send_ref[0, step] = turned_ref[pl.ds(pl.multiple_of((chip + 1 - c) * rows, 16), rows), :].astype(jnp.bfloat16)


def head_combine(where, product, sums, rows_local):
    width, model_width = product.shape
    share = sums.shape[1]
    tile = model_width // 4
    out_spec = pl.BlockSpec((1, 4, rows_local, share), lambda i, s: (i, 0, 0, 0))
    return pl.pallas_call(
        combine_kernel,
        grid_spec=pltpu.PrefetchScalarGridSpec(
            num_scalar_prefetch=1,
            grid=(4,),
            in_specs=[
                pl.BlockSpec((width, tile), lambda i, s: (0, lax.rem(s[0] + i, 4))),
                pl.BlockSpec(sums.shape, lambda i, s: (0, 0)),
            ],
            out_specs=[out_spec, out_spec],
            scratch_shapes=[pltpu.VMEM((tile, share), jnp.float32)],
        ),
        out_shape=[
            jax.ShapeDtypeStruct((4, 4, rows_local, share), jnp.float32),
            jax.ShapeDtypeStruct((4, 4, rows_local, share), jnp.bfloat16),
        ],
        compiler_params=pltpu.CompilerParams(vmem_limit_bytes=wide_vmem),
    )(where, product, sums)


def layer_kernel(place_ref, *refs):
    pieces, (carried_ref, weight_ref, out_ref, full_ref) = refs[:8], refs[8:]
    place(pieces, place_ref, full_ref)
    backward = jnp.dot(weight_ref[0], full_ref[...], preferred_element_type=jnp.float32)
    out_ref[...] = (carried_ref[...].astype(jnp.float32) + backward).astype(jnp.bfloat16)


def layer_back(where, carried, all_weights):
    pieces = tensor_pieces(carried)
    rows_local, model_width = all_weights.shape[1:]
    whole = lambda shape: pl.BlockSpec(shape, lambda i, s: (0,) * len(shape))
    return pl.pallas_call(
        layer_kernel,
        grid_spec=pltpu.PrefetchScalarGridSpec(
            num_scalar_prefetch=1,
            grid=(1,),
            in_specs=[whole(p.shape) for p in pieces]
            + [
                whole(carried.shape),
                pl.BlockSpec((1, rows_local, model_width), lambda i, s: (s[5], 0, 0)),
            ],
            out_specs=whole(carried.shape),
            scratch_shapes=[pltpu.VMEM((model_width, carried.shape[1]), jnp.bfloat16)],
        ),
        out_shape=jax.ShapeDtypeStruct(carried.shape, jnp.bfloat16),
        compiler_params=pltpu.CompilerParams(vmem_limit_bytes=wide_vmem),
    )(where, *pieces, carried, all_weights)


def body(hidden_last, labels, head_weight, layer_inputs, weights, row_state, col_state):
    section_count = lax.axis_size("x")
    section_index = lax.axis_index("x")
    all_rows = labels.shape[0]
    model_width, vocab_local = head_weight.shape
    local_weight = weights[0]
    rows_local = local_weight.shape[0]
    saved_all = layer_inputs[0]
    share = all_rows // section_count
    row_start = section_index * share
    entries = float(model_width * model_width)
    tensor_index = lax.axis_index(("y", "z", "c"))

    def where(layer):
        return jnp.stack(
            [
                lax.axis_index("y"),
                lax.axis_index("z"),
                lax.axis_index("c"),
                tensor_index * vocab_local,
                jnp.int32(all_rows),
                jnp.asarray(layer, jnp.int32),
            ]
        )

    all_weights = lax.all_gather(local_weight, "x", axis=0)
    hidden_rows = lax.dynamic_slice_in_dim(hidden_last, row_start, share, 0).T
    labels_here = lax.dynamic_slice_in_dim(labels, row_start, share, 0)[None, :]
    both, sums = head_logits(where(0), tensor_pieces(hidden_rows), labels_here, head_weight.T)
    sums = summed_tensor(sums)
    product = lax.dot_general(
        both, head_weight, (((0,), (1,)), ((), ())), preferred_element_type=jnp.float32
    )
    keep, send = head_combine(where(0), product, sums, rows_local)
    part = keep + lax.ppermute(send, "c", [(0, 1), (1, 0)]).astype(jnp.float32)
    part = scattered([part[0]] + [part[k].astype(jnp.bfloat16) for k in range(1, 4)], "y")
    part = scattered([part[0]] + [part[k].astype(jnp.bfloat16) for k in range(1, 4)], "z")
    carried = part.astype(jnp.bfloat16)

    def advance(step, state):
        carried, chain = state
        layer = section_count - 1 - step
        carried = layer_back(where(layer), carried, all_weights)
        return carried, lax.dynamic_update_index_in_dim(chain, carried, layer, 0)

    chain = jnp.zeros((section_count + 1, *carried.shape), jnp.bfloat16)
    chain = chain.at[section_count].set(carried)
    carried, chain = lax.fori_loop(0, section_count - 1, advance, (carried, chain))

    dy = exchanged([chain[k + 1] for k in range(section_count)], "x").reshape(rows_local, all_rows)
    dy, carried, local_weight, sums = lax.optimization_barrier((dy, carried, local_weight, sums))
    full = lax.all_gather(dy, ("y", "z", "c"), axis=0, tiled=True)
    carried = layer_back(where(0), carried, all_weights)
    outputs = exchanged([carried] + [chain[k] for k in range(1, section_count)], "x")
    outputs = outputs.reshape(rows_local, all_rows)
    loss = summed(jnp.sum(jnp.log(sums[0]) - sums[1])[None], "x")[0] / all_rows
    gradient = lax.dot_general(
        saved_all, full, (((0,), (1,)), ((), ())), preferred_element_type=jnp.float32
    )

    squares = gradient * gradient
    row_new = decay_rate * row_state[0] + (1.0 - decay_rate) * jnp.mean(squares + tiny_term, axis=1)
    col_part = jnp.sum(squares + tiny_term, axis=0)
    scaled_part = jnp.sum(squares * (1.0 / row_new)[:, None], axis=0)
    weight_float = local_weight.astype(jnp.float32)
    weight_part = jnp.broadcast_to(jnp.sum(weight_float * weight_float), (128,))
    row_part = jnp.broadcast_to(jnp.sum(row_new), (128,))
    payload = jnp.concatenate([col_part, scaled_part, row_part, weight_part]).reshape(-1, 128)
    payload = summed_tensor(payload).reshape(-1)
    col_sum = payload[:model_width]
    scaled_sum = payload[model_width : 2 * model_width]
    row_total = payload[2 * model_width]
    weight_total = payload[2 * model_width + 128]
    col_new = decay_rate * col_state[0] + (1.0 - decay_rate) * (col_sum / model_width)
    update_total = row_total * jnp.sum(scaled_sum / col_new)
    factor = (
        learn_rate
        * jnp.sqrt(weight_total / entries)
        / jnp.maximum(1.0, jnp.sqrt(update_total / entries))
    )
    row_scale = factor * jnp.sqrt(row_total / row_new)
    col_scale = 1.0 / jnp.sqrt(col_new)
    new_weight = (weight_float - gradient * row_scale[:, None] * col_scale[None, :]).astype(jnp.bfloat16)
    return (loss, outputs.T[None], new_weight[None], row_new[None], col_new[None])


def solution(mesh):
    fine = Mesh(mesh.devices.reshape(4, 4, 4, 2), ("x", "y", "z", "c"))
    tensor = ("y", "z", "c")
    return jax.shard_map(
        body,
        mesh=fine,
        in_specs=(
            P(None, tensor),
            P(),
            P(None, tensor),
            P("x", None, tensor),
            P("x", tensor, None),
            P("x", tensor),
            P("x", None),
        ),
        out_specs=(
            P(),
            P("x", None, tensor),
            P("x", tensor, None),
            P("x", tensor),
            P("x", None),
        ),
        check_vma=False,
    )
```

```python
import jax
import jax.numpy as jnp
from jax import lax
from jax.experimental import pallas as pl
from jax.experimental.pallas import tpu as pltpu
from jax.sharding import Mesh, PartitionSpec as P

decay_rate = 0.9
learn_rate = 0.3
tiny_term = 1e-30
bf16_largest = 3.3895e38
wide_vmem = 48 * 1024 * 1024


def from_ring(block, axis):
    size = lax.axis_size(axis)
    return [block] + [
        lax.ppermute(block, axis, [(i, (i - step) % size) for i in range(size)])
        for step in range(1, size)
    ]


def rotated(pieces, index, axis=0):
    count = len(pieces)
    placed = []
    for k in range(count):
        chosen = pieces[k]
        for shift in range(1, count):
            chosen = jnp.where(index == shift, pieces[(k - shift) % count], chosen)
        placed.append(chosen)
    return jnp.stack(placed, axis=axis)


def tensor_pieces(block):
    mine = from_ring(jnp.stack(from_ring(block, "z")), "y")
    return mine + [lax.ppermute(piece, "c", [(0, 1), (1, 0)]) for piece in mine]


def summed(x, axis):
    pieces = from_ring(x, axis)
    if len(pieces) == 2:
        return pieces[0] + pieces[1]
    return (pieces[0] + pieces[2]) + (pieces[1] + pieces[3])


def summed_tensor(x):
    return summed(summed(summed(x, "c"), "z"), "y")


def scattered(blocks, axis):
    size = len(blocks)
    total = blocks[0].astype(jnp.float32)
    for step in range(1, size):
        piece = lax.ppermute(blocks[step], axis, [(i, (i + step) % size) for i in range(size)])
        total = total + piece.astype(jnp.float32)
    return total


def exchanged(blocks, axis):
    size = lax.axis_size(axis)
    index = lax.axis_index(axis)
    pieces = []
    for step in range(size):
        piece = blocks[step]
        for shift in range(1, size):
            piece = jnp.where(index == shift, blocks[(step + shift) % size], piece)
        if step:
            piece = lax.ppermute(piece, axis, [(i, (i + step) % size) for i in range(size)])
        pieces.append(piece)
    return rotated([pieces[-k % size] for k in range(size)], index, 1)


def place(pieces, place_ref, full_ref):
    y, z, c = place_ref[0], place_ref[1], place_ref[2]
    rows = pieces[0].shape[1]
    for side in range(2):
        for step_y in range(4):
            for step_z in range(4):
                chip = lax.rem(y + step_y, 4) * 4 + lax.rem(z + step_z, 4)
                core = c if side == 0 else 1 - c
                start = pl.multiple_of((chip * 2 + core) * rows, 16)
                full_ref[pl.ds(start, rows), :] = pieces[side * 4 + step_y][step_z]


def logits_kernel(place_ref, *refs):
    pieces, (labels_ref, weight_ref, both_ref, sums_ref, full_ref, total_ref) = refs[:8], refs[8:]
    step = pl.program_id(0)
    depth = weight_ref.shape[1]
    share = labels_ref.shape[1]

    @pl.when(step == 0)
    def _():
        place(pieces, place_ref, full_ref)
        total_ref[...] = jnp.zeros_like(total_ref)

    rows = full_ref[pl.ds(pl.multiple_of(step * depth, depth), depth), :]
    total_ref[...] += jnp.dot(weight_ref[...], rows, preferred_element_type=jnp.float32)

    @pl.when(step == pl.num_programs(0) - 1)
    def _():
        logits = total_ref[...]
        exponent = jnp.exp(logits)
        columns = place_ref[3] + lax.broadcasted_iota(jnp.int32, logits.shape, 0)
        label_hit = columns == labels_ref[...]
        sums_ref[0:1, :] = jnp.sum(exponent, axis=0, keepdims=True)
        sums_ref[1:2, :] = jnp.sum(jnp.where(label_hit, logits, 0.0), axis=0, keepdims=True)
        both_ref[:, :share] = jnp.minimum(exponent, bf16_largest).astype(jnp.bfloat16)
        both_ref[:, share:] = jnp.where(label_hit, 1.0, 0.0).astype(jnp.bfloat16)


def head_logits(where, pieces, labels, weight, tile=512):
    vocab_local, model_width = weight.shape
    share = labels.shape[1]
    whole = lambda shape: pl.BlockSpec(shape, lambda i, s: (0,) * len(shape))
    return pl.pallas_call(
        logits_kernel,
        grid_spec=pltpu.PrefetchScalarGridSpec(
            num_scalar_prefetch=1,
            grid=(model_width // tile,),
            in_specs=[whole(p.shape) for p in pieces]
            + [whole(labels.shape), pl.BlockSpec((vocab_local, tile), lambda i, s: (0, i))],
            out_specs=[whole((vocab_local, 2 * share)), whole((2, share))],
            scratch_shapes=[
                pltpu.VMEM((model_width, share), jnp.bfloat16),
                pltpu.VMEM((vocab_local, share), jnp.float32),
            ],
        ),
        out_shape=[
            jax.ShapeDtypeStruct((vocab_local, 2 * share), jnp.bfloat16),
            jax.ShapeDtypeStruct((2, share), jnp.float32),
        ],
        compiler_params=pltpu.CompilerParams(vmem_limit_bytes=wide_vmem),
    )(where, *pieces, labels, weight)


def combine_kernel(place_ref, product_ref, sums_ref, keep_ref, send_ref, turned_ref):
    share = sums_ref.shape[1]
    rows = keep_ref.shape[2]
    z, c = place_ref[1], place_ref[2]
    scale = (1.0 / place_ref[4].astype(jnp.float32)) / sums_ref[0:1, :]
    scale = jnp.broadcast_to(scale, (share, share)).T
    unit = 1.0 / place_ref[4].astype(jnp.float32)
    for at in range(0, product_ref.shape[1], share):
        block = product_ref[:share, at : at + share] * scale - product_ref[share:, at : at + share] * unit
        turned_ref[at : at + share, :] = block.T
    for step in range(4):
        chip = lax.rem(z + step, 4) * 2
        keep_ref[0, step] = turned_ref[pl.ds(pl.multiple_of((chip + c) * rows, 16), rows), :]
        send_ref[0, step] = turned_ref[pl.ds(pl.multiple_of((chip + 1 - c) * rows, 16), rows), :].astype(jnp.bfloat16)


def head_combine(where, product, sums, rows_local):
    width, model_width = product.shape
    share = sums.shape[1]
    tile = model_width // 4
    out_spec = pl.BlockSpec((1, 4, rows_local, share), lambda i, s: (i, 0, 0, 0))
    return pl.pallas_call(
        combine_kernel,
        grid_spec=pltpu.PrefetchScalarGridSpec(
            num_scalar_prefetch=1,
            grid=(4,),
            in_specs=[
                pl.BlockSpec((width, tile), lambda i, s: (0, lax.rem(s[0] + i, 4))),
                pl.BlockSpec(sums.shape, lambda i, s: (0, 0)),
            ],
            out_specs=[out_spec, out_spec],
            scratch_shapes=[pltpu.VMEM((tile, share), jnp.float32)],
        ),
        out_shape=[
            jax.ShapeDtypeStruct((4, 4, rows_local, share), jnp.float32),
            jax.ShapeDtypeStruct((4, 4, rows_local, share), jnp.bfloat16),
        ],
        compiler_params=pltpu.CompilerParams(vmem_limit_bytes=wide_vmem),
    )(where, product, sums)


def layer_kernel(place_ref, *refs):
    pieces, (carried_ref, weight_ref, out_ref, full_ref) = refs[:8], refs[8:]
    place(pieces, place_ref, full_ref)
    backward = jnp.dot(weight_ref[0], full_ref[...], preferred_element_type=jnp.float32)
    out_ref[...] = (carried_ref[...].astype(jnp.float32) + backward).astype(jnp.bfloat16)


def layer_back(where, carried, all_weights):
    pieces = tensor_pieces(carried)
    rows_local, model_width = all_weights.shape[1:]
    whole = lambda shape: pl.BlockSpec(shape, lambda i, s: (0,) * len(shape))
    return pl.pallas_call(
        layer_kernel,
        grid_spec=pltpu.PrefetchScalarGridSpec(
            num_scalar_prefetch=1,
            grid=(1,),
            in_specs=[whole(p.shape) for p in pieces]
            + [
                whole(carried.shape),
                pl.BlockSpec((1, rows_local, model_width), lambda i, s: (s[5], 0, 0)),
            ],
            out_specs=whole(carried.shape),
            scratch_shapes=[pltpu.VMEM((model_width, carried.shape[1]), jnp.bfloat16)],
        ),
        out_shape=jax.ShapeDtypeStruct(carried.shape, jnp.bfloat16),
        compiler_params=pltpu.CompilerParams(vmem_limit_bytes=wide_vmem),
    )(where, *pieces, carried, all_weights)


def statistics_kernel(saved_ref, full_ref, row_ref, weight_ref, gradient_ref, row_new_ref, totals_ref, rows_ref, weights_ref):
    step = pl.program_id(0)
    tile = full_ref.shape[0]
    width = gradient_ref.shape[1]

    def lanes(x):
        return sum(x[:, at : at + 128] for at in range(0, x.shape[1], 128))

    @pl.when(step == 0)
    def _():
        rows_ref[...] = jnp.zeros_like(rows_ref)
        weights_ref[...] = jnp.zeros_like(weights_ref)

    gradient = lax.dot_general(
        saved_ref[...], full_ref[...], (((1,), (1,)), ((), ())), preferred_element_type=jnp.float32
    )
    here = pl.ds(pl.multiple_of(step * tile, tile), tile)
    gradient_ref[:, here] = gradient
    squares = gradient * gradient + tiny_term
    totals_ref[0:1, here] = jnp.sum(squares, axis=0, keepdims=True)
    rows_ref[...] += lanes(squares)
    weight = weight_ref[...].astype(jnp.float32)
    weights_ref[...] += lanes(weight * weight)

    @pl.when(step == pl.num_programs(0) - 1)
    def _():
        mean = jnp.sum(rows_ref[...], axis=1, keepdims=True) / width
        row_new = decay_rate * row_ref[...] + (1.0 - decay_rate) * mean
        row_new_ref[...] = row_new
        inverse = jnp.broadcast_to(1.0 / row_new, rows_ref.shape)
        for at in range(0, width, 128):
            block = gradient_ref[:, at : at + 128]
            totals_ref[1:2, at : at + 128] = jnp.sum(block * block * inverse, axis=0, keepdims=True)
        row_total = jnp.sum(row_new, axis=0, keepdims=True)
        weight_total = jnp.sum(jnp.sum(weights_ref[...], axis=0, keepdims=True), axis=1, keepdims=True)
        totals_ref[0:1, width:] = jnp.broadcast_to(row_total, (1, 128))
        totals_ref[1:2, width:] = jnp.broadcast_to(weight_total, (1, 128))


def gradient_statistics(saved, full, row_state, weight, tile=512):
    rows, tokens = saved.shape
    width = full.shape[0]
    whole = lambda shape: pl.BlockSpec(shape, lambda i: (0,) * len(shape))
    return pl.pallas_call(
        statistics_kernel,
        grid=(width // tile,),
        in_specs=[
            whole(saved.shape),
            pl.BlockSpec((tile, tokens), lambda i: (i, 0)),
            whole(row_state.shape),
            pl.BlockSpec((rows, tile), lambda i: (0, i)),
        ],
        out_specs=[whole((rows, width)), whole((rows, 1)), whole((2, width + 128))],
        out_shape=[
            jax.ShapeDtypeStruct((rows, width), jnp.float32),
            jax.ShapeDtypeStruct((rows, 1), jnp.float32),
            jax.ShapeDtypeStruct((2, width + 128), jnp.float32),
        ],
        scratch_shapes=[pltpu.VMEM((rows, 128), jnp.float32), pltpu.VMEM((rows, 128), jnp.float32)],
        compiler_params=pltpu.CompilerParams(vmem_limit_bytes=wide_vmem),
    )(saved, full, row_state, weight)


def weights_kernel(totals_ref, row_new_ref, col_ref, gradient_ref, weight_ref, out_ref, col_new_ref, rows_ref, cols_ref):
    step = pl.program_id(0)
    tile = weight_ref.shape[1]
    width = col_ref.shape[1]

    @pl.when(step == 0)
    def _():
        entries = float(width) * float(width)
        col_new = decay_rate * col_ref[...] + (1.0 - decay_rate) * (totals_ref[0:1, :width] / width)
        col_new_ref[...] = col_new
        cols_ref[...] = 1.0 / jnp.sqrt(col_new)
        row_total = totals_ref[0:1, width : width + 1]
        weight_total = totals_ref[1:2, width : width + 1]
        update_total = row_total * jnp.sum(totals_ref[1:2, :width] / col_new, axis=1, keepdims=True)
        factor = learn_rate * jnp.sqrt(weight_total / entries)
        factor = factor / jnp.maximum(1.0, jnp.sqrt(update_total / entries))
        rows_ref[...] = jnp.broadcast_to(factor * jnp.sqrt(row_total / row_new_ref[...]), rows_ref.shape)

    for at in range(0, tile, 128):
        here = pl.ds(pl.multiple_of(step * tile + at, 128), 128)
        change = gradient_ref[:, at : at + 128] * rows_ref[...] * cols_ref[:, here]
        weight = weight_ref[:, at : at + 128].astype(jnp.float32)
        out_ref[:, at : at + 128] = (weight - change).astype(jnp.bfloat16)


def updated_weights(totals, row_new, col_state, gradient, weight, tile=512):
    rows, width = weight.shape
    whole = lambda shape: pl.BlockSpec(shape, lambda i: (0,) * len(shape))
    block = pl.BlockSpec((rows, tile), lambda i: (0, i))
    return pl.pallas_call(
        weights_kernel,
        grid=(width // tile,),
        in_specs=[whole(totals.shape), whole(row_new.shape), whole(col_state.shape), block, block],
        out_specs=[block, whole(col_state.shape)],
        out_shape=[
            jax.ShapeDtypeStruct((rows, width), jnp.bfloat16),
            jax.ShapeDtypeStruct(col_state.shape, jnp.float32),
        ],
        scratch_shapes=[pltpu.VMEM((rows, 128), jnp.float32), pltpu.VMEM((1, width), jnp.float32)],
        compiler_params=pltpu.CompilerParams(vmem_limit_bytes=wide_vmem),
    )(totals, row_new, col_state, gradient, weight)


def body(hidden_last, labels, head_weight, layer_inputs, weights, row_state, col_state):
    section_count = lax.axis_size("x")
    section_index = lax.axis_index("x")
    all_rows = labels.shape[0]
    model_width, vocab_local = head_weight.shape
    local_weight = weights[0]
    rows_local = local_weight.shape[0]
    saved_all = layer_inputs[0]
    share = all_rows // section_count
    row_start = section_index * share
    tensor_index = lax.axis_index(("y", "z", "c"))

    def where(layer):
        return jnp.stack(
            [
                lax.axis_index("y"),
                lax.axis_index("z"),
                lax.axis_index("c"),
                tensor_index * vocab_local,
                jnp.int32(all_rows),
                jnp.asarray(layer, jnp.int32),
            ]
        )

    all_weights = lax.all_gather(local_weight, "x", axis=0)
    hidden_rows = lax.dynamic_slice_in_dim(hidden_last, row_start, share, 0).T
    labels_here = lax.dynamic_slice_in_dim(labels, row_start, share, 0)[None, :]
    both, sums = head_logits(where(0), tensor_pieces(hidden_rows), labels_here, head_weight.T)
    sums = summed_tensor(sums)
    product = lax.dot_general(
        both, head_weight, (((0,), (1,)), ((), ())), preferred_element_type=jnp.float32
    )
    keep, send = head_combine(where(0), product, sums, rows_local)
    part = keep + lax.ppermute(send, "c", [(0, 1), (1, 0)]).astype(jnp.float32)
    part = scattered([part[0]] + [part[k].astype(jnp.bfloat16) for k in range(1, 4)], "y")
    part = scattered([part[0]] + [part[k].astype(jnp.bfloat16) for k in range(1, 4)], "z")
    carried = part.astype(jnp.bfloat16)

    chain = [carried]
    for layer in reversed(range(1, section_count)):
        carried = layer_back(where(layer), carried, all_weights)
        chain.insert(0, carried)

    dy = exchanged(chain, "x").reshape(rows_local, all_rows)
    full = lax.all_gather(dy, ("y", "z", "c"), axis=0, tiled=True)
    loss = jnp.sum(jnp.log(sums[0]) - sums[1])[None]
    for distance in (1, 2):
        loss = loss + lax.ppermute(loss, "x", [(i, i ^ distance) for i in range(section_count)])
    loss = loss[0] / all_rows
    full, loss = lax.optimization_barrier((full, loss))
    gradient, row_new, totals = gradient_statistics(saved_all.T, full, row_state.T, local_weight)
    totals = summed_tensor(totals)
    backward = jnp.dot(local_weight, full, preferred_element_type=jnp.float32)
    outputs = (dy.astype(jnp.float32) + backward).astype(jnp.bfloat16)
    new_weight, col_new = updated_weights(totals, row_new, col_state, gradient, local_weight)
    return (loss, outputs.T[None], new_weight[None], row_new.T, col_new)


def solution(mesh):
    fine = Mesh(mesh.devices.reshape(4, 4, 4, 2), ("x", "y", "z", "c"))
    tensor = ("y", "z", "c")
    return jax.shard_map(
        body,
        mesh=fine,
        in_specs=(
            P(None, tensor),
            P(),
            P(None, tensor),
            P("x", None, tensor),
            P("x", tensor, None),
            P("x", tensor),
            P("x", None),
        ),
        out_specs=(
            P(),
            P("x", None, tensor),
            P("x", tensor, None),
            P("x", tensor),
            P("x", None),
        ),
        check_vma=False,
    )
```

```python
import jax
import jax.numpy as jnp
from jax import lax
from jax.experimental import pallas as pl
from jax.experimental.pallas import tpu as pltpu
from jax.sharding import Mesh, PartitionSpec as P

decay_rate = 0.9
learn_rate = 0.3
tiny_term = 1e-30
bf16_largest = 3.3895e38
mebibyte = 1024 * 1024


def from_ring(block, axis):
    size = lax.axis_size(axis)
    return [block] + [
        lax.ppermute(block, axis, [(i, (i - step) % size) for i in range(size)])
        for step in range(1, size)
    ]


def rotated(pieces, index, axis=0):
    count = len(pieces)
    placed = []
    for k in range(count):
        chosen = pieces[k]
        for shift in range(1, count):
            chosen = jnp.where(index == shift, pieces[(k - shift) % count], chosen)
        placed.append(chosen)
    return jnp.stack(placed, axis=axis)


def tensor_pieces(block):
    mine = from_ring(jnp.stack(from_ring(block, "z")), "y")
    return mine + [lax.ppermute(piece, "c", [(0, 1), (1, 0)]) for piece in mine]


def summed(x, axis):
    pieces = from_ring(x, axis)
    if len(pieces) == 2:
        return pieces[0] + pieces[1]
    return (pieces[0] + pieces[2]) + (pieces[1] + pieces[3])


def summed_tensor(x):
    return summed(summed(summed(x, "c"), "z"), "y")


def scattered(blocks, axis):
    size = len(blocks)
    total = blocks[0].astype(jnp.float32)
    for step in range(1, size):
        piece = lax.ppermute(blocks[step], axis, [(i, (i + step) % size) for i in range(size)])
        total = total + piece.astype(jnp.float32)
    return total


def exchanged(blocks, axis):
    size = lax.axis_size(axis)
    index = lax.axis_index(axis)
    pieces = []
    for step in range(size):
        piece = blocks[step]
        for shift in range(1, size):
            piece = jnp.where(index == shift, blocks[(step + shift) % size], piece)
        if step:
            piece = lax.ppermute(piece, axis, [(i, (i + step) % size) for i in range(size)])
        pieces.append(piece)
    return rotated([pieces[-k % size] for k in range(size)], index, 1)


def place(pieces, place_ref, full_ref):
    y, z, c = place_ref[0], place_ref[1], place_ref[2]
    rows = pieces[0].shape[1]
    for side in range(2):
        for step_y in range(4):
            for step_z in range(4):
                chip = lax.rem(y + step_y, 4) * 4 + lax.rem(z + step_z, 4)
                core = c if side == 0 else 1 - c
                start = pl.multiple_of((chip * 2 + core) * rows, 16)
                full_ref[pl.ds(start, rows), :] = pieces[side * 4 + step_y][step_z]


def logits_kernel(place_ref, *refs):
    pieces, (labels_ref, weight_ref, both_ref, sums_ref, full_ref, total_ref) = refs[:8], refs[8:]
    step = pl.program_id(0)
    depth = weight_ref.shape[1]
    share = labels_ref.shape[1]

    @pl.when(step == 0)
    def _():
        place(pieces, place_ref, full_ref)
        total_ref[...] = jnp.zeros_like(total_ref)

    rows = full_ref[pl.ds(pl.multiple_of(step * depth, depth), depth), :]
    total_ref[...] += jnp.dot(weight_ref[...], rows, preferred_element_type=jnp.float32)

    @pl.when(step == pl.num_programs(0) - 1)
    def _():
        logits = total_ref[...]
        exponent = jnp.exp(logits)
        columns = place_ref[3] + lax.broadcasted_iota(jnp.int32, logits.shape, 0)
        label_hit = columns == labels_ref[...]
        sums_ref[0:1, :] = jnp.sum(exponent, axis=0, keepdims=True)
        sums_ref[1:2, :] = jnp.sum(jnp.where(label_hit, logits, 0.0), axis=0, keepdims=True)
        both_ref[:, :share] = jnp.minimum(exponent, bf16_largest).astype(jnp.bfloat16)
        both_ref[:, share:] = jnp.where(label_hit, 1.0, 0.0).astype(jnp.bfloat16)


def head_logits(where, pieces, labels, weight, tile=512):
    vocab_local, model_width = weight.shape
    share = labels.shape[1]
    whole = lambda shape: pl.BlockSpec(shape, lambda i, s: (0,) * len(shape))
    return pl.pallas_call(
        logits_kernel,
        grid_spec=pltpu.PrefetchScalarGridSpec(
            num_scalar_prefetch=1,
            grid=(model_width // tile,),
            in_specs=[whole(p.shape) for p in pieces]
            + [whole(labels.shape), pl.BlockSpec((vocab_local, tile), lambda i, s: (0, i))],
            out_specs=[whole((vocab_local, 2 * share)), whole((2, share))],
            scratch_shapes=[
                pltpu.VMEM((model_width, share), jnp.bfloat16),
                pltpu.VMEM((vocab_local, share), jnp.float32),
            ],
        ),
        out_shape=[
            jax.ShapeDtypeStruct((vocab_local, 2 * share), jnp.bfloat16),
            jax.ShapeDtypeStruct((2, share), jnp.float32),
        ],
        compiler_params=pltpu.CompilerParams(vmem_limit_bytes=48 * mebibyte),
    )(where, *pieces, labels, weight)


def combine_kernel(place_ref, product_ref, sums_ref, keep_ref, send_ref, turned_ref):
    share = sums_ref.shape[1]
    rows = keep_ref.shape[2]
    z, c = place_ref[1], place_ref[2]
    scale = (1.0 / place_ref[4].astype(jnp.float32)) / sums_ref[0:1, :]
    scale = jnp.broadcast_to(scale, (share, share)).T
    unit = 1.0 / place_ref[4].astype(jnp.float32)
    for at in range(0, product_ref.shape[1], share):
        block = product_ref[:share, at : at + share] * scale - product_ref[share:, at : at + share] * unit
        turned_ref[at : at + share, :] = block.T
    for step in range(4):
        chip = lax.rem(z + step, 4) * 2
        keep_ref[0, step] = turned_ref[pl.ds(pl.multiple_of((chip + c) * rows, 16), rows), :]
        send_ref[0, step] = turned_ref[pl.ds(pl.multiple_of((chip + 1 - c) * rows, 16), rows), :].astype(jnp.bfloat16)


def head_combine(where, product, sums, rows_local):
    width, model_width = product.shape
    share = sums.shape[1]
    tile = model_width // 4
    out_spec = pl.BlockSpec((1, 4, rows_local, share), lambda i, s: (i, 0, 0, 0))
    return pl.pallas_call(
        combine_kernel,
        grid_spec=pltpu.PrefetchScalarGridSpec(
            num_scalar_prefetch=1,
            grid=(4,),
            in_specs=[
                pl.BlockSpec((width, tile), lambda i, s: (0, lax.rem(s[0] + i, 4))),
                pl.BlockSpec(sums.shape, lambda i, s: (0, 0)),
            ],
            out_specs=[out_spec, out_spec],
            scratch_shapes=[pltpu.VMEM((tile, share), jnp.float32)],
        ),
        out_shape=[
            jax.ShapeDtypeStruct((4, 4, rows_local, share), jnp.float32),
            jax.ShapeDtypeStruct((4, 4, rows_local, share), jnp.bfloat16),
        ],
        compiler_params=pltpu.CompilerParams(vmem_limit_bytes=48 * mebibyte),
    )(where, product, sums)


def layer_kernel(place_ref, *refs):
    pieces, (carried_ref, weight_ref, out_ref, full_ref) = refs[:8], refs[8:]
    place(pieces, place_ref, full_ref)
    backward = jnp.dot(weight_ref[0], full_ref[...], preferred_element_type=jnp.float32)
    out_ref[...] = (carried_ref[...].astype(jnp.float32) + backward).astype(jnp.bfloat16)


def layer_back(where, carried, all_weights):
    pieces = tensor_pieces(carried)
    rows_local, model_width = all_weights.shape[1:]
    whole = lambda shape: pl.BlockSpec(shape, lambda i, s: (0,) * len(shape))
    return pl.pallas_call(
        layer_kernel,
        grid_spec=pltpu.PrefetchScalarGridSpec(
            num_scalar_prefetch=1,
            grid=(1,),
            in_specs=[whole(p.shape) for p in pieces]
            + [
                whole(carried.shape),
                pl.BlockSpec((1, rows_local, model_width), lambda i, s: (s[5], 0, 0)),
            ],
            out_specs=whole(carried.shape),
            scratch_shapes=[pltpu.VMEM((model_width, carried.shape[1]), jnp.bfloat16)],
        ),
        out_shape=jax.ShapeDtypeStruct(carried.shape, jnp.bfloat16),
        compiler_params=pltpu.CompilerParams(vmem_limit_bytes=48 * mebibyte),
    )(where, *pieces, carried, all_weights)


def fetch_halves(pieces, place_ref, full_ref, sems):
    y, z, c = place_ref[0], place_ref[1], place_ref[2]
    rows, half = pieces[0].shape[1:]
    copies = []
    for number in range(16):
        second, side, outer = number // 8, number // 4 % 2, number % 4
        core = c if side == 0 else 1 - c
        for inner in range(4):
            step_y, step_z = (inner, outer) if second else (outer, inner)
            chip = lax.rem(y + step_y, 4) * 4 + lax.rem(z + step_z, 4)
            start = pl.multiple_of((chip * 2 + core) * rows, 16)
            copies.append(
                pltpu.make_async_copy(
                    pieces[number].at[inner],
                    full_ref.at[pl.ds(start, rows), pl.ds(second * half, half)],
                    sems.at[number, inner],
                )
            )
    for copy in copies:
        copy.start()
    for copy in copies:
        copy.wait()


def all_pieces(halves):
    first = [jnp.stack(from_ring(half, axis)) for half, axis in zip(halves, "zy")]
    first = lax.optimization_barrier(first)

    def fetched(block, axis, step):
        return lax.ppermute(block, axis, [(i, (i - step) % 4) for i in range(4)])

    ahead = [fetched(near, axis, 1) for near, axis in zip(first, "yz")]
    behind = [fetched(near, axis, 3) for near, axis in zip(first, "yz")]
    first, ahead = lax.optimization_barrier((first, ahead))
    across = [fetched(near, axis, 2) for near, axis in zip(first, "yz")]
    pieces = []
    for mine in zip(first, ahead, across, behind):
        pieces += [*mine] + [lax.ppermute(piece, "c", [(0, 1), (1, 0)]) for piece in mine]
    return pieces


def statistics_kernel(place_ref, *refs):
    pieces = refs[:16]
    saved_ref, row_ref, weight_ref, gradient_ref, row_new_ref, totals_ref, full_ref, rows_ref, sems = refs[16:]
    width = gradient_ref.shape[1]
    tile = 512
    fetch_halves(pieces, place_ref, full_ref, sems)
    rows_ref[...] = jnp.zeros_like(rows_ref)

    @pl.loop(0, width // tile)
    def _(step):
        here = pl.ds(pl.multiple_of(step * tile, tile), tile)
        gradient = lax.dot_general(
            saved_ref[...], full_ref[here, :], (((1,), (1,)), ((), ())), preferred_element_type=jnp.float32
        )
        gradient_ref[:, here] = gradient
        squares = gradient * gradient + tiny_term
        totals_ref[0:1, here] = jnp.sum(squares, axis=0, keepdims=True)
        rows_ref[...] += sum(squares[:, at : at + 128] for at in range(0, tile, 128))

    mean = jnp.sum(rows_ref[...], axis=1, keepdims=True) / width
    row_new = decay_rate * row_ref[...] + (1.0 - decay_rate) * mean
    row_new_ref[...] = row_new
    rows_ref[...] = jnp.broadcast_to(1.0 / row_new, rows_ref.shape)

    @pl.loop(0, width // tile)
    def _(step):
        for at in range(0, tile, 128):
            here = pl.ds(pl.multiple_of(step * tile + at, 128), 128)
            block = gradient_ref[:, here]
            totals_ref[1:2, here] = jnp.sum(block * block * rows_ref[...], axis=0, keepdims=True)

    row_total = jnp.sum(row_new, axis=0, keepdims=True)
    totals_ref[0:1, width:] = jnp.broadcast_to(row_total, (1, 128))
    totals_ref[1:2, width:] = jnp.broadcast_to(weight_ref[...], (1, 128))


def gradient_statistics(where, pieces, saved, row_state, weight_part, width):
    rows, tokens = saved.shape
    whole = lambda shape: pl.BlockSpec(shape, lambda i, s: (0,) * len(shape))
    return pl.pallas_call(
        statistics_kernel,
        grid_spec=pltpu.PrefetchScalarGridSpec(
            num_scalar_prefetch=1,
            grid=(1,),
            in_specs=[pl.BlockSpec(memory_space=pl.ANY)] * 16
            + [whole(saved.shape), whole(row_state.shape), whole(weight_part.shape)],
            out_specs=[whole((rows, width)), whole((rows, 1)), whole((2, width + 128))],
            scratch_shapes=[pltpu.VMEM((width, tokens), jnp.bfloat16), pltpu.VMEM((rows, 128), jnp.float32), pltpu.SemaphoreType.DMA((16, 4))],
        ),
        out_shape=[
            jax.ShapeDtypeStruct((rows, width), jnp.float32),
            jax.ShapeDtypeStruct((rows, 1), jnp.float32),
            jax.ShapeDtypeStruct((2, width + 128), jnp.float32),
        ],
        compiler_params=pltpu.CompilerParams(vmem_limit_bytes=48 * mebibyte),
    )(where, *pieces, saved, row_state, weight_part)


def inputs_kernel(place_ref, *refs):
    pieces, (carried_ref, weight_ref, out_ref, full_ref, sems) = refs[:16], refs[16:]
    fetch_halves(pieces, place_ref, full_ref, sems)
    backward = jnp.dot(weight_ref[...], full_ref[...], preferred_element_type=jnp.float32)
    out_ref[...] = (carried_ref[...].astype(jnp.float32) + backward).astype(jnp.bfloat16)


def own_input_grad(where, pieces, carried, weight):
    rows, width = weight.shape
    tokens = carried.shape[1]
    whole = lambda shape: pl.BlockSpec(shape, lambda i, s: (0,) * len(shape))
    return pl.pallas_call(
        inputs_kernel,
        grid_spec=pltpu.PrefetchScalarGridSpec(
            num_scalar_prefetch=1,
            grid=(1,),
            in_specs=[pl.BlockSpec(memory_space=pl.ANY)] * 16 + [whole(carried.shape), whole(weight.shape)],
            out_specs=whole(carried.shape),
            scratch_shapes=[pltpu.VMEM((width, tokens), jnp.bfloat16), pltpu.SemaphoreType.DMA((16, 4))],
        ),
        out_shape=jax.ShapeDtypeStruct(carried.shape, jnp.bfloat16),
        cost_estimate=pl.CostEstimate(
            flops=2 * rows * width * tokens, bytes_accessed=2 * width * (rows + tokens), transcendentals=0
        ),
        compiler_params=pltpu.CompilerParams(vmem_limit_bytes=48 * mebibyte),
    )(where, *pieces, carried, weight)


def weights_kernel(totals_ref, row_new_ref, col_ref, gradient_ref, weight_ref, out_ref, col_new_ref, rows_ref, cols_ref):
    step = pl.program_id(0)
    tile = weight_ref.shape[1]
    width = col_ref.shape[1]

    @pl.when(step == 0)
    def _():
        entries = float(width) * float(width)
        col_new = decay_rate * col_ref[...] + (1.0 - decay_rate) * (totals_ref[0:1, :width] / width)
        col_new_ref[...] = col_new
        cols_ref[...] = 1.0 / jnp.sqrt(col_new)
        row_total = totals_ref[0:1, width : width + 1]
        weight_total = totals_ref[1:2, width : width + 1]
        update_total = row_total * jnp.sum(totals_ref[1:2, :width] / col_new, axis=1, keepdims=True)
        factor = learn_rate * jnp.sqrt(weight_total / entries)
        factor = factor / jnp.maximum(1.0, jnp.sqrt(update_total / entries))
        rows_ref[...] = jnp.broadcast_to(factor * jnp.sqrt(row_total / row_new_ref[...]), rows_ref.shape)

    for at in range(0, tile, 128):
        here = pl.ds(pl.multiple_of(step * tile + at, 128), 128)
        change = gradient_ref[:, at : at + 128] * rows_ref[...] * cols_ref[:, here]
        weight = weight_ref[:, at : at + 128].astype(jnp.float32)
        out_ref[:, at : at + 128] = (weight - change).astype(jnp.bfloat16)


def updated_weights(totals, row_new, col_state, gradient, weight, tile=1664):
    rows, width = weight.shape
    whole = lambda shape: pl.BlockSpec(shape, lambda i: (0,) * len(shape))
    block = pl.BlockSpec((rows, tile), lambda i: (0, i))
    return pl.pallas_call(
        weights_kernel,
        grid=(width // tile,),
        in_specs=[whole(totals.shape), whole(row_new.shape), whole(col_state.shape), block, block],
        out_specs=[block, whole(col_state.shape)],
        out_shape=[
            jax.ShapeDtypeStruct((rows, width), jnp.bfloat16),
            jax.ShapeDtypeStruct(col_state.shape, jnp.float32),
        ],
        scratch_shapes=[pltpu.VMEM((rows, 128), jnp.float32), pltpu.VMEM((1, width), jnp.float32)],
        compiler_params=pltpu.CompilerParams(vmem_limit_bytes=48 * mebibyte),
    )(totals, row_new, col_state, gradient, weight)


def body(hidden_last, labels, head_weight, layer_inputs, weights, row_state, col_state):
    section_count = lax.axis_size("x")
    section_index = lax.axis_index("x")
    all_rows = labels.shape[0]
    model_width, vocab_local = head_weight.shape
    local_weight = weights[0]
    rows_local = local_weight.shape[0]
    saved_all = layer_inputs[0]
    share = all_rows // section_count
    row_start = section_index * share
    tensor_index = lax.axis_index(("y", "z", "c"))

    def where(layer):
        return jnp.stack(
            [
                lax.axis_index("y"),
                lax.axis_index("z"),
                lax.axis_index("c"),
                tensor_index * vocab_local,
                jnp.int32(all_rows),
                jnp.asarray(layer, jnp.int32),
            ]
        )

    all_weights = lax.all_gather(local_weight, "x", axis=0)
    hidden_rows = lax.dynamic_slice_in_dim(hidden_last, row_start, share, 0).T
    labels_here = lax.dynamic_slice_in_dim(labels, row_start, share, 0)[None, :]
    both, sums = head_logits(where(0), tensor_pieces(hidden_rows), labels_here, head_weight.T)
    sums = summed_tensor(sums)
    product = lax.dot_general(
        both, head_weight, (((0,), (1,)), ((), ())), preferred_element_type=jnp.float32
    )
    keep, send = head_combine(where(0), product, sums, rows_local)
    part = keep + lax.ppermute(send, "c", [(0, 1), (1, 0)]).astype(jnp.float32)
    part = scattered([part[0]] + [part[k].astype(jnp.bfloat16) for k in range(1, 4)], "y")
    part = scattered([part[0]] + [part[k].astype(jnp.bfloat16) for k in range(1, 4)], "z")
    carried = part.astype(jnp.bfloat16)

    chain = [carried]
    for layer in reversed(range(1, section_count)):
        carried = layer_back(where(layer), carried, all_weights)
        chain.insert(0, carried)

    dy = exchanged(chain, "x").reshape(rows_local, all_rows)
    pieces = all_pieces([dy[:, : all_rows // 2], dy[:, all_rows // 2 :]])
    loss = jnp.sum(jnp.log(sums[0]) - sums[1])[None]
    for distance in (1, 2):
        loss = loss + lax.ppermute(loss, "x", [(i, i ^ distance) for i in range(section_count)])
    loss = loss[0] / all_rows
    weight_float = local_weight.astype(jnp.float32)
    weight_part = jnp.sum(weight_float * weight_float).reshape(1, 1)
    pieces, loss, weight_part = lax.optimization_barrier((pieces, loss, weight_part))
    gradient, row_new, totals = gradient_statistics(
        where(0), pieces, saved_all.T, row_state.T, weight_part, model_width
    )
    totals = summed_tensor(totals)
    outputs = own_input_grad(where(0), pieces, dy, local_weight)
    new_weight, col_new = updated_weights(totals, row_new, col_state, gradient, local_weight)
    return (loss, outputs.T[None], new_weight[None], row_new.T, col_new)


def solution(mesh):
    fine = Mesh(mesh.devices.reshape(4, 4, 4, 2), ("x", "y", "z", "c"))
    tensor = ("y", "z", "c")
    return jax.shard_map(
        body,
        mesh=fine,
        in_specs=(
            P(None, tensor),
            P(),
            P(None, tensor),
            P("x", None, tensor),
            P("x", tensor, None),
            P("x", tensor),
            P("x", None),
        ),
        out_specs=(
            P(),
            P("x", None, tensor),
            P("x", tensor, None),
            P("x", tensor),
            P("x", None),
        ),
        check_vma=False,
    )
```

```python
import jax
import jax.numpy as jnp
from jax import lax
from jax.experimental import pallas as pl
from jax.experimental.pallas import tpu as pltpu
from jax.sharding import Mesh, PartitionSpec as P

decay_rate = 0.9
learn_rate = 0.3
tiny_term = 1e-30
bf16_largest = 3.3895e38
chips = ("y", "z")
wide_vmem = 48 * 1024 * 1024


def rotated(pieces, index, axis=0):
    count = len(pieces)
    placed = []
    for k in range(count):
        chosen = pieces[k]
        for shift in range(1, count):
            chosen = jnp.where(index == shift, pieces[(k - shift) % count], chosen)
        placed.append(chosen)
    return jnp.stack(placed, axis=axis)


def other_core(x):
    return lax.ppermute(x, "c", [(0, 1), (1, 0)])


def swapped_chips(blocks):
    return lax.all_to_all(blocks, chips, 0, 0, tiled=True)


def from_chips(block):
    count = lax.axis_size(chips)
    return swapped_chips(jnp.broadcast_to(block[None], (count, *block.shape)))


def tensor_pieces(block):
    mine = from_chips(block)
    return [mine, other_core(mine)]


def summed_tensor(x):
    return jnp.sum(from_chips(x + other_core(x)), axis=0)


def exchanged(blocks, axis):
    size = lax.axis_size(axis)
    index = lax.axis_index(axis)
    pieces = []
    for step in range(size):
        piece = blocks[step]
        for shift in range(1, size):
            piece = jnp.where(index == shift, blocks[(step + shift) % size], piece)
        if step:
            piece = lax.ppermute(piece, axis, [(i, (i + step) % size) for i in range(size)])
        pieces.append(piece)
    return rotated([pieces[-k % size] for k in range(size)], index, 1)


def place(pieces, place_ref, full_ref):
    c = place_ref[2]
    count, rows = pieces[0].shape[:2]
    for chip in range(count):
        for side in range(2):
            core = c if side == 0 else 1 - c
            start = pl.multiple_of((chip * 2 + core) * rows, 16)
            full_ref[pl.ds(start, rows), :] = pieces[side][chip]


def logits_kernel(place_ref, *refs):
    pieces, (labels_ref, weight_ref, both_ref, sums_ref, full_ref, total_ref) = refs[:2], refs[2:]
    step = pl.program_id(0)
    depth = weight_ref.shape[1]
    share = labels_ref.shape[1]

    @pl.when(step == 0)
    def _():
        place(pieces, place_ref, full_ref)
        total_ref[...] = jnp.zeros_like(total_ref)

    rows = full_ref[pl.ds(pl.multiple_of(step * depth, depth), depth), :]
    total_ref[...] += jnp.dot(weight_ref[...], rows, preferred_element_type=jnp.float32)

    @pl.when(step == pl.num_programs(0) - 1)
    def _():
        logits = total_ref[...]
        exponent = jnp.exp(logits)
        columns = place_ref[3] + lax.broadcasted_iota(jnp.int32, logits.shape, 0)
        label_hit = columns == labels_ref[...]
        sums_ref[0:1, :] = jnp.sum(exponent, axis=0, keepdims=True)
        sums_ref[1:2, :] = jnp.sum(jnp.where(label_hit, logits, 0.0), axis=0, keepdims=True)
        both_ref[:, :share] = jnp.minimum(exponent, bf16_largest).astype(jnp.bfloat16)
        both_ref[:, share:] = jnp.where(label_hit, 1.0, 0.0).astype(jnp.bfloat16)


def head_logits(where, pieces, labels, weight, tile=512):
    vocab_local, model_width = weight.shape
    share = labels.shape[1]
    whole = lambda shape: pl.BlockSpec(shape, lambda i, s: (0,) * len(shape))
    return pl.pallas_call(
        logits_kernel,
        grid_spec=pltpu.PrefetchScalarGridSpec(
            num_scalar_prefetch=1,
            grid=(model_width // tile,),
            in_specs=[whole(p.shape) for p in pieces]
            + [whole(labels.shape), pl.BlockSpec((vocab_local, tile), lambda i, s: (0, i))],
            out_specs=[whole((vocab_local, 2 * share)), whole((2, share))],
            scratch_shapes=[
                pltpu.VMEM((model_width, share), jnp.bfloat16),
                pltpu.VMEM((vocab_local, share), jnp.float32),
            ],
        ),
        out_shape=[
            jax.ShapeDtypeStruct((vocab_local, 2 * share), jnp.bfloat16),
            jax.ShapeDtypeStruct((2, share), jnp.float32),
        ],
        compiler_params=pltpu.CompilerParams(vmem_limit_bytes=wide_vmem),
    )(where, *pieces, labels, weight)


def combine_kernel(place_ref, product_ref, sums_ref, keep_ref, send_ref, turned_ref):
    share = sums_ref.shape[1]
    rows = keep_ref.shape[2]
    c = place_ref[2]
    scale = (1.0 / place_ref[4].astype(jnp.float32)) / sums_ref[0:1, :]
    scale = jnp.broadcast_to(scale, (share, share)).T
    unit = 1.0 / place_ref[4].astype(jnp.float32)
    for at in range(0, product_ref.shape[1], share):
        block = product_ref[:share, at : at + share] * scale - product_ref[share:, at : at + share] * unit
        turned_ref[at : at + share, :] = block.T
    for step in range(4):
        chip = step * 2
        keep_ref[0, step] = turned_ref[pl.ds(pl.multiple_of((chip + c) * rows, 16), rows), :]
        send_ref[0, step] = turned_ref[pl.ds(pl.multiple_of((chip + 1 - c) * rows, 16), rows), :].astype(jnp.bfloat16)


def head_combine(where, product, sums, rows_local):
    width, model_width = product.shape
    share = sums.shape[1]
    tile = model_width // 4
    out_spec = pl.BlockSpec((1, 4, rows_local, share), lambda i, s: (i, 0, 0, 0))
    return pl.pallas_call(
        combine_kernel,
        grid_spec=pltpu.PrefetchScalarGridSpec(
            num_scalar_prefetch=1,
            grid=(4,),
            in_specs=[
                pl.BlockSpec((width, tile), lambda i, s: (0, i)),
                pl.BlockSpec(sums.shape, lambda i, s: (0, 0)),
            ],
            out_specs=[out_spec, out_spec],
            scratch_shapes=[pltpu.VMEM((tile, share), jnp.float32)],
        ),
        out_shape=[
            jax.ShapeDtypeStruct((4, 4, rows_local, share), jnp.float32),
            jax.ShapeDtypeStruct((4, 4, rows_local, share), jnp.bfloat16),
        ],
        compiler_params=pltpu.CompilerParams(vmem_limit_bytes=wide_vmem),
    )(where, product, sums)


def layer_kernel(place_ref, *refs):
    pieces, (carried_ref, weight_ref, out_ref, full_ref) = refs[:2], refs[2:]
    place(pieces, place_ref, full_ref)
    backward = jnp.dot(weight_ref[0], full_ref[...], preferred_element_type=jnp.float32)
    out_ref[...] = (carried_ref[...].astype(jnp.float32) + backward).astype(jnp.bfloat16)


def layer_back(where, carried, all_weights):
    pieces = tensor_pieces(carried)
    rows_local, model_width = all_weights.shape[1:]
    whole = lambda shape: pl.BlockSpec(shape, lambda i, s: (0,) * len(shape))
    return pl.pallas_call(
        layer_kernel,
        grid_spec=pltpu.PrefetchScalarGridSpec(
            num_scalar_prefetch=1,
            grid=(1,),
            in_specs=[whole(p.shape) for p in pieces]
            + [
                whole(carried.shape),
                pl.BlockSpec((1, rows_local, model_width), lambda i, s: (s[5], 0, 0)),
            ],
            out_specs=whole(carried.shape),
            scratch_shapes=[pltpu.VMEM((model_width, carried.shape[1]), jnp.bfloat16)],
        ),
        out_shape=jax.ShapeDtypeStruct(carried.shape, jnp.bfloat16),
        compiler_params=pltpu.CompilerParams(vmem_limit_bytes=wide_vmem),
    )(where, *pieces, carried, all_weights)


def weights_kernel(totals_ref, row_new_ref, col_ref, gradient_ref, weight_ref, out_ref, col_new_ref, rows_ref, cols_ref):
    step = pl.program_id(0)
    tile = weight_ref.shape[1]
    width = col_ref.shape[1]

    @pl.when(step == 0)
    def _():
        entries = float(width) * float(width)
        col_new = decay_rate * col_ref[...] + (1.0 - decay_rate) * (totals_ref[0:1, :width] / width)
        col_new_ref[...] = col_new
        cols_ref[...] = 1.0 / jnp.sqrt(col_new)
        row_total = totals_ref[0:1, width : width + 1]
        weight_total = totals_ref[1:2, width : width + 1]
        update_total = row_total * jnp.sum(totals_ref[1:2, :width] / col_new, axis=1, keepdims=True)
        factor = learn_rate * jnp.sqrt(weight_total / entries)
        factor = factor / jnp.maximum(1.0, jnp.sqrt(update_total / entries))
        rows_ref[...] = jnp.broadcast_to(factor * jnp.sqrt(row_total / row_new_ref[...]), rows_ref.shape)

    for at in range(0, tile, 128):
        here = pl.ds(pl.multiple_of(step * tile + at, 128), 128)
        change = gradient_ref[:, at : at + 128] * rows_ref[...] * cols_ref[:, here]
        weight = weight_ref[:, at : at + 128].astype(jnp.float32)
        out_ref[:, at : at + 128] = (weight - change).astype(jnp.bfloat16)


def updated_weights(totals, row_new, col_state, gradient, weight, tile=1664):
    rows, width = weight.shape
    whole = lambda shape: pl.BlockSpec(shape, lambda i: (0,) * len(shape))
    block = pl.BlockSpec((rows, tile), lambda i: (0, i))
    return pl.pallas_call(
        weights_kernel,
        grid=(width // tile,),
        in_specs=[whole(totals.shape), whole(row_new.shape), whole(col_state.shape), block, block],
        out_specs=[block, whole(col_state.shape)],
        out_shape=[
            jax.ShapeDtypeStruct((rows, width), jnp.bfloat16),
            jax.ShapeDtypeStruct(col_state.shape, jnp.float32),
        ],
        scratch_shapes=[pltpu.VMEM((rows, 128), jnp.float32), pltpu.VMEM((1, width), jnp.float32)],
        compiler_params=pltpu.CompilerParams(vmem_limit_bytes=wide_vmem),
    )(totals, row_new, col_state, gradient, weight)


def body(hidden_last, labels, head_weight, layer_inputs, weights, row_state, col_state):
    section_count = lax.axis_size("x")
    section_index = lax.axis_index("x")
    all_rows = labels.shape[0]
    model_width, vocab_local = head_weight.shape
    local_weight = weights[0]
    rows_local = local_weight.shape[0]
    saved_all = layer_inputs[0]
    share = all_rows // section_count
    row_start = section_index * share
    tensor_index = lax.axis_index(("y", "z", "c"))

    def where(layer):
        return jnp.stack(
            [
                lax.axis_index("y"),
                lax.axis_index("z"),
                lax.axis_index("c"),
                tensor_index * vocab_local,
                jnp.int32(all_rows),
                jnp.asarray(layer, jnp.int32),
            ]
        )

    all_weights = lax.all_gather(local_weight, "x", axis=0)
    hidden_rows = lax.dynamic_slice_in_dim(hidden_last, row_start, share, 0).T
    labels_here = lax.dynamic_slice_in_dim(labels, row_start, share, 0)[None, :]
    both, sums = head_logits(where(0), tensor_pieces(hidden_rows), labels_here, head_weight.T)
    sums = summed_tensor(sums)
    product = lax.dot_general(
        both, head_weight, (((0,), (1,)), ((), ())), preferred_element_type=jnp.float32
    )
    keep, send = head_combine(where(0), product, sums, rows_local)
    part = (keep + other_core(send).astype(jnp.float32)).astype(jnp.bfloat16)
    part = swapped_chips(part.reshape(-1, rows_local, share)).astype(jnp.float32).sum(axis=0)
    carried = part.astype(jnp.bfloat16)

    chain = [carried]
    for layer in reversed(range(1, section_count)):
        carried = layer_back(where(layer), carried, all_weights)
        chain.insert(0, carried)

    dy = exchanged(chain, "x").reshape(rows_local, all_rows)
    full = lax.all_gather(dy, ("y", "z", "c"), axis=0, tiled=True)
    loss = jnp.sum(jnp.log(sums[0]) - sums[1])[None]
    for distance in (1, 2):
        loss = loss + lax.ppermute(loss, "x", [(i, i ^ distance) for i in range(section_count)])
    loss = loss[0] / all_rows
    weight_float = local_weight.astype(jnp.float32)
    weight_part = jnp.broadcast_to(jnp.sum(weight_float * weight_float), (128,))
    full, loss, weight_part = lax.optimization_barrier((full, loss, weight_part))
    gradient = lax.dot_general(
        saved_all, full, (((0,), (1,)), ((), ())), preferred_element_type=jnp.float32
    )
    squares = gradient * gradient
    row_new = decay_rate * row_state[0] + (1.0 - decay_rate) * jnp.mean(squares + tiny_term, axis=1)
    col_part = jnp.sum(squares + tiny_term, axis=0)
    scaled_part = jnp.sum(squares * (1.0 / row_new)[:, None], axis=0)
    row_part = jnp.broadcast_to(jnp.sum(row_new), (128,))
    totals = jnp.stack(
        [jnp.concatenate([col_part, row_part]), jnp.concatenate([scaled_part, weight_part])]
    )
    totals = summed_tensor(totals)
    row_new = row_new[:, None]
    backward = jnp.dot(local_weight, full, preferred_element_type=jnp.float32)
    outputs = (dy.astype(jnp.float32) + backward).astype(jnp.bfloat16)
    new_weight, col_new = updated_weights(totals, row_new, col_state, gradient, local_weight)
    return (loss, outputs.T[None], new_weight[None], row_new.T, col_new)


def solution(mesh):
    fine = Mesh(mesh.devices.reshape(4, 4, 4, 2), ("x", "y", "z", "c"))
    tensor = ("y", "z", "c")
    return jax.shard_map(
        body,
        mesh=fine,
        in_specs=(
            P(None, tensor),
            P(),
            P(None, tensor),
            P("x", None, tensor),
            P("x", tensor, None),
            P("x", tensor),
            P("x", None),
        ),
        out_specs=(
            P(),
            P("x", None, tensor),
            P("x", tensor, None),
            P("x", tensor),
            P("x", None),
        ),
        check_vma=False,
    )
```

```python
import jax
import jax.numpy as jnp
from jax import lax
from jax.experimental import pallas as pl
from jax.experimental.pallas import tpu as pltpu
from jax.sharding import Mesh, PartitionSpec as P

decay_rate = 0.9
learn_rate = 0.3
tiny_term = 1e-30
bf16_largest = 3.3895e38
chips = ("y", "z")
wide_vmem = 48 * 1024 * 1024


def rotated(pieces, index, axis=0):
    count = len(pieces)
    placed = []
    for k in range(count):
        chosen = pieces[k]
        for shift in range(1, count):
            chosen = jnp.where(index == shift, pieces[(k - shift) % count], chosen)
        placed.append(chosen)
    return jnp.stack(placed, axis=axis)


def other_core(x):
    return lax.ppermute(x, "c", [(0, 1), (1, 0)])


def swapped_chips(blocks):
    return lax.all_to_all(blocks, chips, 0, 0, tiled=True)


def from_chips(block):
    count = lax.axis_size(chips)
    return swapped_chips(jnp.broadcast_to(block[None], (count, *block.shape)))


def tensor_pieces(block):
    mine = from_chips(block)
    return [mine, other_core(mine)]


def summed_tensor(x):
    return jnp.sum(from_chips(x + other_core(x)), axis=0)


def summed_ring(x, axis):
    one, two, three = (
        lax.ppermute(x, axis, [(i, (i - step) % 4) for i in range(4)]) for step in (1, 2, 3)
    )
    return (x + two) + (one + three)


def exchanged(blocks, axis):
    size = lax.axis_size(axis)
    index = lax.axis_index(axis)
    pieces = []
    for step in range(size):
        piece = blocks[step]
        for shift in range(1, size):
            piece = jnp.where(index == shift, blocks[(step + shift) % size], piece)
        if step:
            piece = lax.ppermute(piece, axis, [(i, (i + step) % size) for i in range(size)])
        pieces.append(piece)
    return rotated([pieces[-k % size] for k in range(size)], index, 1)


def place(pieces, place_ref, full_ref):
    c = place_ref[2]
    count, rows = pieces[0].shape[:2]
    for chip in range(count):
        for side in range(2):
            core = c if side == 0 else 1 - c
            start = pl.multiple_of((chip * 2 + core) * rows, 16)
            full_ref[pl.ds(start, rows), :] = pieces[side][chip]


def order_kernel(place_ref, *refs):
    place(refs[:2], place_ref, refs[2])


def in_order(where, pieces):
    count, rows, tokens = pieces[0].shape
    whole = lambda shape: pl.BlockSpec(shape, lambda i, s: (0,) * len(shape))
    return pl.pallas_call(
        order_kernel,
        grid_spec=pltpu.PrefetchScalarGridSpec(
            num_scalar_prefetch=1,
            grid=(1,),
            in_specs=[whole(p.shape) for p in pieces],
            out_specs=whole((2 * count * rows, tokens)),
        ),
        out_shape=jax.ShapeDtypeStruct((2 * count * rows, tokens), jnp.bfloat16),
        compiler_params=pltpu.CompilerParams(vmem_limit_bytes=wide_vmem),
    )(where, *pieces)


def combine_kernel(place_ref, product_ref, sums_ref, keep_ref, send_ref, turned_ref):
    share = sums_ref.shape[1]
    rows = keep_ref.shape[2]
    c = place_ref[2]
    scale = (1.0 / place_ref[4].astype(jnp.float32)) / sums_ref[0:1, :]
    scale = jnp.broadcast_to(scale, (share, share)).T
    unit = 1.0 / place_ref[4].astype(jnp.float32)
    for at in range(0, product_ref.shape[1], share):
        block = product_ref[:share, at : at + share] * scale - product_ref[share:, at : at + share] * unit
        turned_ref[at : at + share, :] = block.T
    for step in range(4):
        chip = step * 2
        keep_ref[0, step] = turned_ref[pl.ds(pl.multiple_of((chip + c) * rows, 16), rows), :]
        send_ref[0, step] = turned_ref[pl.ds(pl.multiple_of((chip + 1 - c) * rows, 16), rows), :].astype(jnp.bfloat16)


def head_combine(where, product, sums, rows_local):
    width, model_width = product.shape
    share = sums.shape[1]
    tile = model_width // 4
    out_spec = pl.BlockSpec((1, 4, rows_local, share), lambda i, s: (i, 0, 0, 0))
    return pl.pallas_call(
        combine_kernel,
        grid_spec=pltpu.PrefetchScalarGridSpec(
            num_scalar_prefetch=1,
            grid=(4,),
            in_specs=[
                pl.BlockSpec((width, tile), lambda i, s: (0, i)),
                pl.BlockSpec(sums.shape, lambda i, s: (0, 0)),
            ],
            out_specs=[out_spec, out_spec],
            scratch_shapes=[pltpu.VMEM((tile, share), jnp.float32)],
        ),
        out_shape=[
            jax.ShapeDtypeStruct((4, 4, rows_local, share), jnp.float32),
            jax.ShapeDtypeStruct((4, 4, rows_local, share), jnp.bfloat16),
        ],
        compiler_params=pltpu.CompilerParams(vmem_limit_bytes=wide_vmem),
    )(where, product, sums)


def layer_kernel(place_ref, *refs):
    pieces, (carried_ref, weight_ref, out_ref, full_ref) = refs[:2], refs[2:]
    place(pieces, place_ref, full_ref)
    backward = jnp.dot(weight_ref[0], full_ref[...], preferred_element_type=jnp.float32)
    out_ref[...] = (carried_ref[...].astype(jnp.float32) + backward).astype(jnp.bfloat16)


def layer_back(where, carried, all_weights):
    pieces = tensor_pieces(carried)
    rows_local, model_width = all_weights.shape[1:]
    whole = lambda shape: pl.BlockSpec(shape, lambda i, s: (0,) * len(shape))
    return pl.pallas_call(
        layer_kernel,
        grid_spec=pltpu.PrefetchScalarGridSpec(
            num_scalar_prefetch=1,
            grid=(1,),
            in_specs=[whole(p.shape) for p in pieces]
            + [
                whole(carried.shape),
                pl.BlockSpec((1, rows_local, model_width), lambda i, s: (s[5], 0, 0)),
            ],
            out_specs=whole(carried.shape),
            scratch_shapes=[pltpu.VMEM((model_width, carried.shape[1]), jnp.bfloat16)],
        ),
        out_shape=jax.ShapeDtypeStruct(carried.shape, jnp.bfloat16),
        compiler_params=pltpu.CompilerParams(vmem_limit_bytes=wide_vmem),
    )(where, *pieces, carried, all_weights)


def weights_kernel(totals_ref, row_new_ref, col_ref, gradient_ref, weight_ref, out_ref, col_new_ref, rows_ref, cols_ref):
    step = pl.program_id(0)
    tile = weight_ref.shape[1]
    width = col_ref.shape[1]

    @pl.when(step == 0)
    def _():
        entries = float(width) * float(width)
        col_new = decay_rate * col_ref[...] + (1.0 - decay_rate) * (totals_ref[0:1, :width] / width)
        col_new_ref[...] = col_new
        cols_ref[...] = 1.0 / jnp.sqrt(col_new)
        row_total = totals_ref[0:1, width : width + 1]
        weight_total = totals_ref[1:2, width : width + 1]
        update_total = row_total * jnp.sum(totals_ref[1:2, :width] / col_new, axis=1, keepdims=True)
        factor = learn_rate * jnp.sqrt(weight_total / entries)
        factor = factor / jnp.maximum(1.0, jnp.sqrt(update_total / entries))
        rows_ref[...] = jnp.broadcast_to(factor * jnp.sqrt(row_total / row_new_ref[...]), rows_ref.shape)

    for at in range(0, tile, 128):
        here = pl.ds(pl.multiple_of(step * tile + at, 128), 128)
        change = gradient_ref[:, at : at + 128] * rows_ref[...] * cols_ref[:, here]
        weight = weight_ref[:, at : at + 128].astype(jnp.float32)
        out_ref[:, at : at + 128] = (weight - change).astype(jnp.bfloat16)


def updated_weights(totals, row_new, col_state, gradient, weight, tile=1664):
    rows, width = weight.shape
    whole = lambda shape: pl.BlockSpec(shape, lambda i: (0,) * len(shape))
    block = pl.BlockSpec((rows, tile), lambda i: (0, i))
    return pl.pallas_call(
        weights_kernel,
        grid=(width // tile,),
        in_specs=[whole(totals.shape), whole(row_new.shape), whole(col_state.shape), block, block],
        out_specs=[block, whole(col_state.shape)],
        out_shape=[
            jax.ShapeDtypeStruct((rows, width), jnp.bfloat16),
            jax.ShapeDtypeStruct(col_state.shape, jnp.float32),
        ],
        scratch_shapes=[pltpu.VMEM((rows, 128), jnp.float32), pltpu.VMEM((1, width), jnp.float32)],
        compiler_params=pltpu.CompilerParams(vmem_limit_bytes=wide_vmem),
    )(totals, row_new, col_state, gradient, weight)


def body(hidden_last, labels, head_weight, layer_inputs, weights, row_state, col_state):
    section_count = lax.axis_size("x")
    section_index = lax.axis_index("x")
    all_rows = labels.shape[0]
    model_width, vocab_local = head_weight.shape
    local_weight = weights[0]
    rows_local = local_weight.shape[0]
    saved_all = layer_inputs[0]
    share = all_rows // section_count
    row_start = section_index * share
    tensor_index = lax.axis_index(("y", "z", "c"))

    def where(layer):
        return jnp.stack(
            [
                lax.axis_index("y"),
                lax.axis_index("z"),
                lax.axis_index("c"),
                tensor_index * vocab_local,
                jnp.int32(all_rows),
                jnp.asarray(layer, jnp.int32),
            ]
        )

    all_weights = lax.all_gather(local_weight, "x", axis=0)
    hidden_rows = lax.dynamic_slice_in_dim(hidden_last, row_start, share, 0).T
    labels_here = lax.dynamic_slice_in_dim(labels, row_start, share, 0)
    hidden_all = in_order(where(0), tensor_pieces(hidden_rows))
    logits = lax.dot_general(
        head_weight, hidden_all, (((0,), (0,)), ((), ())), preferred_element_type=jnp.float32
    )
    exponent = jnp.exp(logits)
    columns = tensor_index * vocab_local + lax.iota(jnp.int32, vocab_local)
    label_hit = labels_here[None, :] == columns[:, None]
    sums = jnp.stack(
        [
            jnp.sum(exponent, axis=0),
            jnp.sum(jnp.where(label_hit, logits, jnp.zeros_like(logits)), axis=0),
        ]
    )
    sums = summed_tensor(sums)
    both = jnp.concatenate(
        [jnp.minimum(exponent, bf16_largest).astype(jnp.bfloat16), label_hit.astype(jnp.bfloat16)], axis=1
    )
    product = lax.dot_general(
        both, head_weight, (((0,), (1,)), ((), ())), preferred_element_type=jnp.float32
    )
    keep, send = head_combine(where(0), product, sums, rows_local)
    part = (keep + other_core(send).astype(jnp.float32)).astype(jnp.bfloat16)
    part = swapped_chips(part.reshape(-1, rows_local, share)).astype(jnp.float32).sum(axis=0)
    carried = part.astype(jnp.bfloat16)

    chain = [carried]
    for layer in reversed(range(1, section_count)):
        carried = layer_back(where(layer), carried, all_weights)
        chain.insert(0, carried)

    dy = exchanged(chain, "x").reshape(rows_local, all_rows)
    full = lax.all_gather(dy, ("y", "z", "c"), axis=0, tiled=True)
    loss = jnp.sum(jnp.log(sums[0]) - sums[1])[None]
    for distance in (1, 2):
        loss = loss + lax.ppermute(loss, "x", [(i, i ^ distance) for i in range(section_count)])
    loss = loss[0] / all_rows
    weight_float = local_weight.astype(jnp.float32)
    weight_part = jnp.broadcast_to(jnp.sum(weight_float * weight_float), (128,))
    full, loss, weight_part = lax.optimization_barrier((full, loss, weight_part))
    gradient = lax.dot_general(
        saved_all, full, (((0,), (1,)), ((), ())), preferred_element_type=jnp.float32
    )
    squares = gradient * gradient
    row_new = decay_rate * row_state[0] + (1.0 - decay_rate) * jnp.mean(squares + tiny_term, axis=1)
    col_part = jnp.sum(squares + tiny_term, axis=0)
    scaled_part = jnp.sum(squares * (1.0 / row_new)[:, None], axis=0)
    row_part = jnp.broadcast_to(jnp.sum(row_new), (128,))
    totals = jnp.stack(
        [jnp.concatenate([col_part, row_part]), jnp.concatenate([scaled_part, weight_part])]
    )
    totals = totals + other_core(totals)
    totals = summed_ring(summed_ring(totals, "z"), "y")
    row_new = row_new[:, None]
    backward = jnp.dot(local_weight, full, preferred_element_type=jnp.float32)
    outputs = (dy.astype(jnp.float32) + backward).astype(jnp.bfloat16)
    new_weight, col_new = updated_weights(totals, row_new, col_state, gradient, local_weight)
    return (loss, outputs.T[None], new_weight[None], row_new.T, col_new)


def solution(mesh):
    fine = Mesh(mesh.devices.reshape(4, 4, 4, 2), ("x", "y", "z", "c"))
    tensor = ("y", "z", "c")
    return jax.shard_map(
        body,
        mesh=fine,
        in_specs=(
            P(None, tensor),
            P(),
            P(None, tensor),
            P("x", None, tensor),
            P("x", tensor, None),
            P("x", tensor),
            P("x", None),
        ),
        out_specs=(
            P(),
            P("x", None, tensor),
            P("x", tensor, None),
            P("x", tensor),
            P("x", None),
        ),
        check_vma=False,
    )
```

```python
import jax
import jax.numpy as jnp
from jax import lax
from jax.experimental import pallas as pl
from jax.experimental.pallas import tpu as pltpu
from jax.sharding import Mesh, PartitionSpec as P

decay_rate = 0.9
learn_rate = 0.3
tiny_term = 1e-30
bf16_largest = 3.3895e38
chips = ("y", "z")
wide_vmem = 48 * 1024 * 1024


def rotated(pieces, index, axis=0):
    count = len(pieces)
    placed = []
    for k in range(count):
        chosen = pieces[k]
        for shift in range(1, count):
            chosen = jnp.where(index == shift, pieces[(k - shift) % count], chosen)
        placed.append(chosen)
    return jnp.stack(placed, axis=axis)


def other_core(x):
    return lax.ppermute(x, "c", [(0, 1), (1, 0)])


def swapped_chips(blocks):
    return lax.all_to_all(blocks, chips, 0, 0, tiled=True)


def from_chips(block):
    count = lax.axis_size(chips)
    return swapped_chips(jnp.broadcast_to(block[None], (count, *block.shape)))


def tensor_pieces(block):
    mine = from_chips(block)
    return [mine, other_core(mine)]


def summed_tensor(x):
    return jnp.sum(from_chips(x + other_core(x)), axis=0)


def summed_ring(x, axis):
    one, two, three = (
        lax.ppermute(x, axis, [(i, (i - step) % 4) for i in range(4)]) for step in (1, 2, 3)
    )
    return (x + two) + (one + three)


def exchanged(blocks, axis):
    size = lax.axis_size(axis)
    index = lax.axis_index(axis)
    pieces = []
    for step in range(size):
        piece = blocks[step]
        for shift in range(1, size):
            piece = jnp.where(index == shift, blocks[(step + shift) % size], piece)
        if step:
            piece = lax.ppermute(piece, axis, [(i, (i + step) % size) for i in range(size)])
        pieces.append(piece)
    return rotated([pieces[-k % size] for k in range(size)], index, 1)


def place(pieces, place_ref, full_ref):
    c = place_ref[2]
    count, rows = pieces[0].shape[:2]
    for chip in range(count):
        for side in range(2):
            core = c if side == 0 else 1 - c
            start = pl.multiple_of((chip * 2 + core) * rows, 16)
            full_ref[pl.ds(start, rows), :] = pieces[side][chip]


def order_kernel(place_ref, *refs):
    place(refs[:2], place_ref, refs[2])


def in_order(where, pieces):
    count, rows, tokens = pieces[0].shape
    whole = lambda shape: pl.BlockSpec(shape, lambda i, s: (0,) * len(shape))
    return pl.pallas_call(
        order_kernel,
        grid_spec=pltpu.PrefetchScalarGridSpec(
            num_scalar_prefetch=1,
            grid=(1,),
            in_specs=[whole(p.shape) for p in pieces],
            out_specs=whole((2 * count * rows, tokens)),
        ),
        out_shape=jax.ShapeDtypeStruct((2 * count * rows, tokens), jnp.bfloat16),
        compiler_params=pltpu.CompilerParams(vmem_limit_bytes=wide_vmem),
    )(where, *pieces)


def combine_kernel(place_ref, product_ref, sums_ref, keep_ref, send_ref, turned_ref):
    share = sums_ref.shape[1]
    rows = keep_ref.shape[2]
    c = place_ref[2]
    scale = (1.0 / place_ref[4].astype(jnp.float32)) / sums_ref[0:1, :]
    scale = jnp.broadcast_to(scale, (share, share)).T
    unit = 1.0 / place_ref[4].astype(jnp.float32)
    for at in range(0, product_ref.shape[1], share):
        block = product_ref[:share, at : at + share] * scale - product_ref[share:, at : at + share] * unit
        turned_ref[at : at + share, :] = block.T
    for step in range(4):
        chip = step * 2
        keep_ref[0, step] = turned_ref[pl.ds(pl.multiple_of((chip + c) * rows, 16), rows), :]
        send_ref[0, step] = turned_ref[pl.ds(pl.multiple_of((chip + 1 - c) * rows, 16), rows), :].astype(jnp.bfloat16)


def head_combine(where, product, sums, rows_local):
    width, model_width = product.shape
    share = sums.shape[1]
    tile = model_width // 4
    out_spec = pl.BlockSpec((1, 4, rows_local, share), lambda i, s: (i, 0, 0, 0))
    return pl.pallas_call(
        combine_kernel,
        grid_spec=pltpu.PrefetchScalarGridSpec(
            num_scalar_prefetch=1,
            grid=(4,),
            in_specs=[
                pl.BlockSpec((width, tile), lambda i, s: (0, i)),
                pl.BlockSpec(sums.shape, lambda i, s: (0, 0)),
            ],
            out_specs=[out_spec, out_spec],
            scratch_shapes=[pltpu.VMEM((tile, share), jnp.float32)],
        ),
        out_shape=[
            jax.ShapeDtypeStruct((4, 4, rows_local, share), jnp.float32),
            jax.ShapeDtypeStruct((4, 4, rows_local, share), jnp.bfloat16),
        ],
        compiler_params=pltpu.CompilerParams(vmem_limit_bytes=wide_vmem),
    )(where, product, sums)


def layer_kernel(place_ref, *refs):
    pieces, (carried_ref, weight_ref, out_ref, full_ref) = refs[:2], refs[2:]
    place(pieces, place_ref, full_ref)
    total = carried_ref[...].astype(jnp.float32)
    quarter = weight_ref.shape[2]
    for part in range(weight_ref.shape[0]):
        rows = full_ref[part * quarter : (part + 1) * quarter, :]
        total = total + jnp.dot(weight_ref[part], rows, preferred_element_type=jnp.float32)
    out_ref[...] = total.astype(jnp.bfloat16)


def layer_back(where, carried, weight):
    pieces = tensor_pieces(carried)
    width = weight.shape[0] * weight.shape[2]
    whole = lambda shape: pl.BlockSpec(shape, lambda i, s: (0,) * len(shape))
    return pl.pallas_call(
        layer_kernel,
        grid_spec=pltpu.PrefetchScalarGridSpec(
            num_scalar_prefetch=1,
            grid=(1,),
            in_specs=[whole(p.shape) for p in pieces] + [whole(carried.shape), whole(weight.shape)],
            out_specs=whole(carried.shape),
            scratch_shapes=[pltpu.VMEM((width, carried.shape[1]), jnp.bfloat16)],
        ),
        out_shape=jax.ShapeDtypeStruct(carried.shape, jnp.bfloat16),
        compiler_params=pltpu.CompilerParams(vmem_limit_bytes=wide_vmem),
    )(where, *pieces, carried, weight)


def weights_kernel(totals_ref, row_new_ref, col_ref, gradient_ref, weight_ref, out_ref, col_new_ref, rows_ref, cols_ref):
    step = pl.program_id(0)
    tile = weight_ref.shape[1]
    width = col_ref.shape[1]

    @pl.when(step == 0)
    def _():
        entries = float(width) * float(width)
        col_new = decay_rate * col_ref[...] + (1.0 - decay_rate) * (totals_ref[0:1, :width] / width)
        col_new_ref[...] = col_new
        cols_ref[...] = 1.0 / jnp.sqrt(col_new)
        row_total = totals_ref[0:1, width : width + 1]
        weight_total = totals_ref[1:2, width : width + 1]
        update_total = row_total * jnp.sum(totals_ref[1:2, :width] / col_new, axis=1, keepdims=True)
        factor = learn_rate * jnp.sqrt(weight_total / entries)
        factor = factor / jnp.maximum(1.0, jnp.sqrt(update_total / entries))
        rows_ref[...] = jnp.broadcast_to(factor * jnp.sqrt(row_total / row_new_ref[...]), rows_ref.shape)

    for at in range(0, tile, 128):
        here = pl.ds(pl.multiple_of(step * tile + at, 128), 128)
        change = gradient_ref[:, at : at + 128] * rows_ref[...] * cols_ref[:, here]
        weight = weight_ref[:, at : at + 128].astype(jnp.float32)
        out_ref[:, at : at + 128] = (weight - change).astype(jnp.bfloat16)


def updated_weights(totals, row_new, col_state, gradient, weight, tile=1664):
    rows, width = weight.shape
    whole = lambda shape: pl.BlockSpec(shape, lambda i: (0,) * len(shape))
    block = pl.BlockSpec((rows, tile), lambda i: (0, i))
    return pl.pallas_call(
        weights_kernel,
        grid=(width // tile,),
        in_specs=[whole(totals.shape), whole(row_new.shape), whole(col_state.shape), block, block],
        out_specs=[block, whole(col_state.shape)],
        out_shape=[
            jax.ShapeDtypeStruct((rows, width), jnp.bfloat16),
            jax.ShapeDtypeStruct(col_state.shape, jnp.float32),
        ],
        scratch_shapes=[pltpu.VMEM((rows, 128), jnp.float32), pltpu.VMEM((1, width), jnp.float32)],
        compiler_params=pltpu.CompilerParams(vmem_limit_bytes=wide_vmem),
    )(totals, row_new, col_state, gradient, weight)


def body(hidden_last, labels, head_weight, layer_inputs, weights, row_state, col_state):
    section_count = lax.axis_size("x")
    section_index = lax.axis_index("x")
    all_rows = labels.shape[0]
    model_width, vocab_local = head_weight.shape
    local_weight = weights[0]
    rows_local = local_weight.shape[0]
    saved_all = layer_inputs[0]
    share = all_rows // section_count
    row_start = section_index * share
    tensor_index = lax.axis_index(("y", "z", "c"))

    def where(layer):
        return jnp.stack(
            [
                lax.axis_index("y"),
                lax.axis_index("z"),
                lax.axis_index("c"),
                tensor_index * vocab_local,
                jnp.int32(all_rows),
                jnp.asarray(layer, jnp.int32),
            ]
        )

    quarter = model_width // section_count
    last = section_count - 1
    own_last = local_weight[:, last * quarter :]
    parts_last = []
    for step in range(1, section_count):
        target = (last + step) % section_count
        part = local_weight[:, target * quarter : (target + 1) * quarter]
        parts_last.append(lax.ppermute(part, "x", [(last, target)]))
    hidden_rows = lax.dynamic_slice_in_dim(hidden_last, row_start, share, 0).T
    labels_here = lax.dynamic_slice_in_dim(labels, row_start, share, 0)
    hidden_chips, parts_last = lax.optimization_barrier((from_chips(hidden_rows), parts_last))
    part = own_last
    for target in range(last):
        part = jnp.where(section_index == target, parts_last[target], part)
    all_weights = {last: lax.all_gather(part, "x", axis=0)}
    hidden_all = in_order(where(0), [hidden_chips, other_core(hidden_chips)])
    logits = lax.dot_general(
        head_weight, hidden_all, (((0,), (0,)), ((), ())), preferred_element_type=jnp.float32
    )
    exponent = jnp.exp(logits)
    columns = tensor_index * vocab_local + lax.iota(jnp.int32, vocab_local)
    label_hit = labels_here[None, :] == columns[:, None]
    sums = jnp.stack(
        [
            jnp.sum(exponent, axis=0),
            jnp.sum(jnp.where(label_hit, logits, jnp.zeros_like(logits)), axis=0),
        ]
    )
    sums = summed_tensor(sums)
    both = jnp.concatenate(
        [jnp.minimum(exponent, bf16_largest).astype(jnp.bfloat16), label_hit.astype(jnp.bfloat16)], axis=1
    )
    product = lax.dot_general(
        both, head_weight, (((0,), (1,)), ((), ())), preferred_element_type=jnp.float32
    )
    keep, send = head_combine(where(0), product, sums, rows_local)
    part = (keep + other_core(send).astype(jnp.float32)).astype(jnp.bfloat16)
    part = swapped_chips(part.reshape(-1, rows_local, share)).astype(jnp.float32).sum(axis=0)
    carried = part.astype(jnp.bfloat16)

    held = []
    for step in range(section_count):
        start = (section_index + step) % section_count * quarter
        part = lax.dynamic_slice_in_dim(local_weight, start, quarter, 1)
        if step:
            part = lax.ppermute(part, "x", [(i, (i + step) % section_count) for i in range(1, last)])
        held.append(part)
    held, carried = lax.optimization_barrier((held, carried))
    for layer in reversed(range(1, last)):
        part = held[0]
        for step in range(1, section_count):
            part = jnp.where(section_index == (layer + step) % section_count, held[step], part)
        all_weights[layer] = lax.all_gather(part, "x", axis=0)

    chain = [carried]
    for layer in reversed(range(1, section_count)):
        carried = layer_back(where(layer), carried, all_weights[layer])
        chain.insert(0, carried)

    dy = exchanged(chain, "x").reshape(rows_local, all_rows)
    full = lax.all_gather(dy, ("y", "z", "c"), axis=0, tiled=True)
    loss = jnp.sum(jnp.log(sums[0]) - sums[1])[None]
    for distance in (1, 2):
        loss = loss + lax.ppermute(loss, "x", [(i, i ^ distance) for i in range(section_count)])
    loss = loss[0] / all_rows
    weight_float = local_weight.astype(jnp.float32)
    weight_part = jnp.broadcast_to(jnp.sum(weight_float * weight_float), (128,))
    full, loss, weight_part = lax.optimization_barrier((full, loss, weight_part))
    gradient = lax.dot_general(
        saved_all, full, (((0,), (1,)), ((), ())), preferred_element_type=jnp.float32
    )
    squares = gradient * gradient
    row_new = decay_rate * row_state[0] + (1.0 - decay_rate) * jnp.mean(squares + tiny_term, axis=1)
    col_part = jnp.sum(squares + tiny_term, axis=0)
    scaled_part = jnp.sum(squares * (1.0 / row_new)[:, None], axis=0)
    row_part = jnp.broadcast_to(jnp.sum(row_new), (128,))
    totals = jnp.stack(
        [jnp.concatenate([col_part, row_part]), jnp.concatenate([scaled_part, weight_part])]
    )
    totals = totals + other_core(totals)
    totals = summed_ring(summed_ring(totals, "z"), "y")
    row_new = row_new[:, None]
    backward = jnp.dot(local_weight, full, preferred_element_type=jnp.float32)
    outputs = (dy.astype(jnp.float32) + backward).astype(jnp.bfloat16)
    new_weight, col_new = updated_weights(totals, row_new, col_state, gradient, local_weight)
    return (loss, outputs.T[None], new_weight[None], row_new.T, col_new)


def solution(mesh):
    fine = Mesh(mesh.devices.reshape(4, 4, 4, 2), ("x", "y", "z", "c"))
    tensor = ("y", "z", "c")
    return jax.shard_map(
        body,
        mesh=fine,
        in_specs=(
            P(None, tensor),
            P(),
            P(None, tensor),
            P("x", None, tensor),
            P("x", tensor, None),
            P("x", tensor),
            P("x", None),
        ),
        out_specs=(
            P(),
            P("x", None, tensor),
            P("x", tensor, None),
            P("x", tensor),
            P("x", None),
        ),
        check_vma=False,
    )
```

```python
import jax
import jax.numpy as jnp
from jax import lax
from jax.experimental import pallas as pl
from jax.experimental.pallas import tpu as pltpu
from jax.sharding import Mesh, PartitionSpec as P

decay_rate = 0.9
learn_rate = 0.3
tiny_term = 1e-30
bf16_largest = 3.3895e38
chips = ("y", "z")
wide_vmem = 48 * 1024 * 1024


def rotated(pieces, index, axis=0):
    count = len(pieces)
    placed = []
    for k in range(count):
        chosen = pieces[k]
        for shift in range(1, count):
            chosen = jnp.where(index == shift, pieces[(k - shift) % count], chosen)
        placed.append(chosen)
    return jnp.stack(placed, axis=axis)


def other_core(x):
    return lax.ppermute(x, "c", [(0, 1), (1, 0)])


def swapped_chips(blocks):
    return lax.all_to_all(blocks, chips, 0, 0, tiled=True)


def from_chips(block):
    count = lax.axis_size(chips)
    return swapped_chips(jnp.broadcast_to(block[None], (count, *block.shape)))


def tensor_pieces(block):
    mine = from_chips(block)
    return [mine, other_core(mine)]


def summed_tensor(x):
    return jnp.sum(from_chips(x + other_core(x)), axis=0)


def summed_ring(x, axis):
    one, two, three = (
        lax.ppermute(x, axis, [(i, (i - step) % 4) for i in range(4)]) for step in (1, 2, 3)
    )
    return (x + two) + (one + three)


def exchanged(blocks, axis):
    size = lax.axis_size(axis)
    index = lax.axis_index(axis)
    pieces = []
    for step in range(size):
        piece = blocks[step]
        for shift in range(1, size):
            piece = jnp.where(index == shift, blocks[(step + shift) % size], piece)
        if step:
            piece = lax.ppermute(piece, axis, [(i, (i + step) % size) for i in range(size)])
        pieces.append(piece)
    return rotated([pieces[-k % size] for k in range(size)], index, 1)


def place(pieces, place_ref, full_ref):
    c = place_ref[2]
    count, rows = pieces[0].shape[:2]
    for chip in range(count):
        for side in range(2):
            core = c if side == 0 else 1 - c
            start = pl.multiple_of((chip * 2 + core) * rows, 16)
            full_ref[pl.ds(start, rows), :] = pieces[side][chip]


def order_kernel(place_ref, *refs):
    place(refs[:2], place_ref, refs[2])


def in_order(where, pieces):
    count, rows, tokens = pieces[0].shape
    whole = lambda shape: pl.BlockSpec(shape, lambda i, s: (0,) * len(shape))
    return pl.pallas_call(
        order_kernel,
        grid_spec=pltpu.PrefetchScalarGridSpec(
            num_scalar_prefetch=1,
            grid=(1,),
            in_specs=[whole(p.shape) for p in pieces],
            out_specs=whole((2 * count * rows, tokens)),
        ),
        out_shape=jax.ShapeDtypeStruct((2 * count * rows, tokens), jnp.bfloat16),
        compiler_params=pltpu.CompilerParams(vmem_limit_bytes=wide_vmem),
    )(where, *pieces)


def combine_kernel(place_ref, product_ref, sums_ref, keep_ref, send_ref, turned_ref):
    share = sums_ref.shape[1]
    rows = keep_ref.shape[2]
    c = place_ref[2]
    scale = (1.0 / place_ref[4].astype(jnp.float32)) / sums_ref[0:1, :]
    scale = jnp.broadcast_to(scale, (share, share)).T
    unit = 1.0 / place_ref[4].astype(jnp.float32)
    for at in range(0, product_ref.shape[1], share):
        block = product_ref[:share, at : at + share] * scale - product_ref[share:, at : at + share] * unit
        turned_ref[at : at + share, :] = block.T
    for step in range(4):
        chip = step * 2
        keep_ref[0, step] = turned_ref[pl.ds(pl.multiple_of((chip + c) * rows, 16), rows), :]
        send_ref[0, step] = turned_ref[pl.ds(pl.multiple_of((chip + 1 - c) * rows, 16), rows), :].astype(jnp.bfloat16)


def head_combine(where, product, sums, rows_local):
    width, model_width = product.shape
    share = sums.shape[1]
    tile = model_width // 4
    out_spec = pl.BlockSpec((1, 4, rows_local, share), lambda i, s: (i, 0, 0, 0))
    return pl.pallas_call(
        combine_kernel,
        grid_spec=pltpu.PrefetchScalarGridSpec(
            num_scalar_prefetch=1,
            grid=(4,),
            in_specs=[
                pl.BlockSpec((width, tile), lambda i, s: (0, i)),
                pl.BlockSpec(sums.shape, lambda i, s: (0, 0)),
            ],
            out_specs=[out_spec, out_spec],
            scratch_shapes=[pltpu.VMEM((tile, share), jnp.float32)],
        ),
        out_shape=[
            jax.ShapeDtypeStruct((4, 4, rows_local, share), jnp.float32),
            jax.ShapeDtypeStruct((4, 4, rows_local, share), jnp.bfloat16),
        ],
        compiler_params=pltpu.CompilerParams(vmem_limit_bytes=wide_vmem),
    )(where, product, sums)


def layer_kernel(place_ref, *refs):
    pieces, (carried_ref, weight_ref, out_ref, full_ref) = refs[:2], refs[2:]
    place(pieces, place_ref, full_ref)
    backward = jnp.dot(weight_ref[0], full_ref[...], preferred_element_type=jnp.float32)
    out_ref[...] = (carried_ref[...].astype(jnp.float32) + backward).astype(jnp.bfloat16)


def layer_back(where, carried, all_weights):
    pieces = tensor_pieces(carried)
    rows_local, model_width = all_weights.shape[1:]
    whole = lambda shape: pl.BlockSpec(shape, lambda i, s: (0,) * len(shape))
    return pl.pallas_call(
        layer_kernel,
        grid_spec=pltpu.PrefetchScalarGridSpec(
            num_scalar_prefetch=1,
            grid=(1,),
            in_specs=[whole(p.shape) for p in pieces]
            + [
                whole(carried.shape),
                pl.BlockSpec((1, rows_local, model_width), lambda i, s: (s[5], 0, 0)),
            ],
            out_specs=whole(carried.shape),
            scratch_shapes=[pltpu.VMEM((model_width, carried.shape[1]), jnp.bfloat16)],
        ),
        out_shape=jax.ShapeDtypeStruct(carried.shape, jnp.bfloat16),
        compiler_params=pltpu.CompilerParams(vmem_limit_bytes=wide_vmem),
    )(where, *pieces, carried, all_weights)


def weights_kernel(totals_ref, row_new_ref, col_ref, gradient_ref, weight_ref, out_ref, col_new_ref, rows_ref, cols_ref):
    step = pl.program_id(0)
    tile = weight_ref.shape[1]
    width = col_ref.shape[1]

    @pl.when(step == 0)
    def _():
        entries = float(width) * float(width)
        col_new = decay_rate * col_ref[...] + (1.0 - decay_rate) * (totals_ref[0:1, :width] / width)
        col_new_ref[...] = col_new
        cols_ref[...] = 1.0 / jnp.sqrt(col_new)
        row_total = totals_ref[0:1, width : width + 1]
        weight_total = totals_ref[1:2, width : width + 1]
        update_total = row_total * jnp.sum(totals_ref[1:2, :width] / col_new, axis=1, keepdims=True)
        factor = learn_rate * jnp.sqrt(weight_total / entries)
        factor = factor / jnp.maximum(1.0, jnp.sqrt(update_total / entries))
        rows_ref[...] = jnp.broadcast_to(factor * jnp.sqrt(row_total / row_new_ref[...]), rows_ref.shape)

    for at in range(0, tile, 128):
        here = pl.ds(pl.multiple_of(step * tile + at, 128), 128)
        change = gradient_ref[:, at : at + 128].astype(jnp.float32) * rows_ref[...] * cols_ref[:, here]
        weight = weight_ref[:, at : at + 128].astype(jnp.float32)
        out_ref[:, at : at + 128] = (weight - change).astype(jnp.bfloat16)


def updated_weights(totals, row_new, col_state, gradient, weight, tile=1664):
    rows, width = weight.shape
    whole = lambda shape: pl.BlockSpec(shape, lambda i: (0,) * len(shape))
    block = pl.BlockSpec((rows, tile), lambda i: (0, i))
    return pl.pallas_call(
        weights_kernel,
        grid=(width // tile,),
        in_specs=[whole(totals.shape), whole(row_new.shape), whole(col_state.shape), block, block],
        out_specs=[block, whole(col_state.shape)],
        out_shape=[
            jax.ShapeDtypeStruct((rows, width), jnp.bfloat16),
            jax.ShapeDtypeStruct(col_state.shape, jnp.float32),
        ],
        scratch_shapes=[pltpu.VMEM((rows, 128), jnp.float32), pltpu.VMEM((1, width), jnp.float32)],
        compiler_params=pltpu.CompilerParams(vmem_limit_bytes=60 * 1024 * 1024),
    )(totals, row_new, col_state, gradient, weight)


def body(hidden_last, labels, head_weight, layer_inputs, weights, row_state, col_state):
    section_count = lax.axis_size("x")
    section_index = lax.axis_index("x")
    all_rows = labels.shape[0]
    model_width, vocab_local = head_weight.shape
    local_weight = weights[0]
    rows_local = local_weight.shape[0]
    saved_all = layer_inputs[0]
    share = all_rows // section_count
    row_start = section_index * share
    tensor_index = lax.axis_index(("y", "z", "c"))

    def where(layer):
        return jnp.stack(
            [
                lax.axis_index("y"),
                lax.axis_index("z"),
                lax.axis_index("c"),
                tensor_index * vocab_local,
                jnp.int32(all_rows),
                jnp.asarray(layer, jnp.int32),
            ]
        )

    all_weights = lax.all_gather(local_weight, "x", axis=0)
    hidden_rows = lax.dynamic_slice_in_dim(hidden_last, row_start, share, 0).T
    labels_here = lax.dynamic_slice_in_dim(labels, row_start, share, 0)
    hidden_all = in_order(where(0), tensor_pieces(hidden_rows))
    logits = lax.dot_general(
        head_weight, hidden_all, (((0,), (0,)), ((), ())), preferred_element_type=jnp.float32
    )
    exponent = jnp.exp(logits)
    columns = tensor_index * vocab_local + lax.iota(jnp.int32, vocab_local)
    label_hit = labels_here[None, :] == columns[:, None]
    sums = jnp.stack(
        [
            jnp.sum(exponent, axis=0),
            jnp.sum(jnp.where(label_hit, logits, jnp.zeros_like(logits)), axis=0),
        ]
    )
    sums = summed_tensor(sums)
    both = jnp.concatenate(
        [jnp.minimum(exponent, bf16_largest).astype(jnp.bfloat16), label_hit.astype(jnp.bfloat16)], axis=1
    )
    product = lax.dot_general(
        both, head_weight, (((0,), (1,)), ((), ())), preferred_element_type=jnp.float32
    )
    keep, send = head_combine(where(0), product, sums, rows_local)
    part = (keep + other_core(send).astype(jnp.float32)).astype(jnp.bfloat16)
    part = swapped_chips(part.reshape(-1, rows_local, share)).astype(jnp.float32).sum(axis=0)
    carried = part.astype(jnp.bfloat16)

    chain = [carried]
    for layer in reversed(range(1, section_count)):
        carried = layer_back(where(layer), carried, all_weights)
        chain.insert(0, carried)

    dy = exchanged(chain, "x").reshape(rows_local, all_rows)
    full = lax.all_gather(dy, ("y", "z", "c"), axis=0, tiled=True)
    loss = jnp.sum(jnp.log(sums[0]) - sums[1])[None]
    for distance in (1, 2):
        loss = loss + lax.ppermute(loss, "x", [(i, i ^ distance) for i in range(section_count)])
    loss = loss[0] / all_rows
    weight_float = local_weight.astype(jnp.float32)
    weight_part = jnp.sum(weight_float * weight_float)
    full, loss, weight_part = lax.optimization_barrier((full, loss, weight_part))
    gradient = lax.dot_general(
        saved_all, full, (((0,), (1,)), ((), ())), preferred_element_type=jnp.float32
    )
    row_mean = jnp.mean(gradient * gradient + tiny_term, axis=1)
    gradient = gradient.astype(jnp.bfloat16)
    squares = jnp.square(gradient.astype(jnp.float32))
    row_new = decay_rate * row_state[0] + (1.0 - decay_rate) * row_mean
    col_part = jnp.sum(squares + tiny_term, axis=0)
    scaled_part = jnp.sum(squares * (1.0 / row_new)[:, None], axis=0)
    room = [(0, 128, 0)]
    totals = jnp.stack([lax.pad(col_part, jnp.sum(row_new), room), lax.pad(scaled_part, weight_part, room)])
    totals = totals + other_core(totals)
    totals = summed_ring(summed_ring(totals, "z"), "y")
    row_new = row_new[:, None]
    backward = jnp.dot(local_weight, full, preferred_element_type=jnp.float32)
    outputs = (dy.astype(jnp.float32) + backward).astype(jnp.bfloat16)
    new_weight, col_new = updated_weights(totals, row_new, col_state, gradient, local_weight)
    return (loss, outputs.T[None], new_weight[None], row_new.T, col_new)


def solution(mesh):
    fine = Mesh(mesh.devices.reshape(4, 4, 4, 2), ("x", "y", "z", "c"))
    tensor = ("y", "z", "c")
    return jax.shard_map(
        body,
        mesh=fine,
        in_specs=(
            P(None, tensor),
            P(),
            P(None, tensor),
            P("x", None, tensor),
            P("x", tensor, None),
            P("x", tensor),
            P("x", None),
        ),
        out_specs=(
            P(),
            P("x", None, tensor),
            P("x", tensor, None),
            P("x", tensor),
            P("x", None),
        ),
        check_vma=False,
    )
```

```python
import jax
import jax.numpy as jnp
from jax import lax
from jax.experimental import pallas as pl
from jax.experimental.pallas import tpu as pltpu
from jax.sharding import Mesh, PartitionSpec as P

decay_rate = 0.9
learn_rate = 0.3
tiny_term = 1e-30
bf16_largest = 3.3895e38
chips = ("y", "z")
wide_vmem = 48 * 1024 * 1024


def rotated(pieces, index, axis=0):
    count = len(pieces)
    placed = []
    for k in range(count):
        chosen = pieces[k]
        for shift in range(1, count):
            chosen = jnp.where(index == shift, pieces[(k - shift) % count], chosen)
        placed.append(chosen)
    return jnp.stack(placed, axis=axis)


def other_core(x):
    return lax.ppermute(x, "c", [(0, 1), (1, 0)])


def swapped_chips(blocks):
    return lax.all_to_all(blocks, chips, 0, 0, tiled=True)


def from_chips(block):
    count = lax.axis_size(chips)
    return swapped_chips(jnp.broadcast_to(block[None], (count, *block.shape)))


def tensor_pieces(block):
    mine = from_chips(block)
    return [mine, other_core(mine)]


def summed_tensor(x):
    return jnp.sum(from_chips(x + other_core(x)), axis=0)


def summed_ring(x, axis):
    one, two, three = (
        lax.ppermute(x, axis, [(i, (i - step) % 4) for i in range(4)]) for step in (1, 2, 3)
    )
    return (x + two) + (one + three)


def exchanged(blocks, axis):
    size = lax.axis_size(axis)
    index = lax.axis_index(axis)
    pieces = []
    for step in range(size):
        piece = blocks[step]
        for shift in range(1, size):
            piece = jnp.where(index == shift, blocks[(step + shift) % size], piece)
        if step:
            piece = lax.ppermute(piece, axis, [(i, (i + step) % size) for i in range(size)])
        pieces.append(piece)
    return rotated([pieces[-k % size] for k in range(size)], index, 1)


def place(pieces, place_ref, full_ref):
    c = place_ref[2]
    count, rows = pieces[0].shape[:2]
    for chip in range(count):
        for side in range(2):
            core = c if side == 0 else 1 - c
            start = pl.multiple_of((chip * 2 + core) * rows, 16)
            full_ref[pl.ds(start, rows), :] = pieces[side][chip]


def order_kernel(place_ref, *refs):
    place(refs[:2], place_ref, refs[2])


def in_order(where, pieces):
    count, rows, tokens = pieces[0].shape
    whole = lambda shape: pl.BlockSpec(shape, lambda i, s: (0,) * len(shape))
    return pl.pallas_call(
        order_kernel,
        grid_spec=pltpu.PrefetchScalarGridSpec(
            num_scalar_prefetch=1,
            grid=(1,),
            in_specs=[whole(p.shape) for p in pieces],
            out_specs=whole((2 * count * rows, tokens)),
        ),
        out_shape=jax.ShapeDtypeStruct((2 * count * rows, tokens), jnp.bfloat16),
        compiler_params=pltpu.CompilerParams(vmem_limit_bytes=wide_vmem),
    )(where, *pieces)


def combine_kernel(place_ref, product_ref, sums_ref, keep_ref, send_ref, turned_ref):
    share = sums_ref.shape[1]
    rows = keep_ref.shape[2]
    c = place_ref[2]
    scale = (1.0 / place_ref[4].astype(jnp.float32)) / sums_ref[0:1, :]
    scale = jnp.broadcast_to(scale, (share, share)).T
    unit = 1.0 / place_ref[4].astype(jnp.float32)
    for at in range(0, product_ref.shape[1], share):
        block = product_ref[:share, at : at + share] * scale - product_ref[share:, at : at + share] * unit
        turned_ref[at : at + share, :] = block.T
    for step in range(4):
        chip = step * 2
        keep_ref[0, step] = turned_ref[pl.ds(pl.multiple_of((chip + c) * rows, 16), rows), :]
        send_ref[0, step] = turned_ref[pl.ds(pl.multiple_of((chip + 1 - c) * rows, 16), rows), :].astype(jnp.bfloat16)


def head_combine(where, product, sums, rows_local):
    width, model_width = product.shape
    share = sums.shape[1]
    tile = model_width // 4
    out_spec = pl.BlockSpec((1, 4, rows_local, share), lambda i, s: (i, 0, 0, 0))
    return pl.pallas_call(
        combine_kernel,
        grid_spec=pltpu.PrefetchScalarGridSpec(
            num_scalar_prefetch=1,
            grid=(4,),
            in_specs=[
                pl.BlockSpec((width, tile), lambda i, s: (0, i)),
                pl.BlockSpec(sums.shape, lambda i, s: (0, 0)),
            ],
            out_specs=[out_spec, out_spec],
            scratch_shapes=[pltpu.VMEM((tile, share), jnp.float32)],
        ),
        out_shape=[
            jax.ShapeDtypeStruct((4, 4, rows_local, share), jnp.float32),
            jax.ShapeDtypeStruct((4, 4, rows_local, share), jnp.bfloat16),
        ],
        compiler_params=pltpu.CompilerParams(vmem_limit_bytes=wide_vmem),
    )(where, product, sums)


def layer_kernel(place_ref, *refs):
    pieces, (carried_ref, weight_ref, out_ref, full_ref, total_ref) = refs[:2], refs[2:]
    step = pl.program_id(0)
    depth = weight_ref.shape[2]

    @pl.when(step == 0)
    def _():
        place(pieces, place_ref, full_ref)
        total_ref[...] = carried_ref[...].astype(jnp.float32)

    rows = full_ref[pl.ds(pl.multiple_of(step * depth, depth), depth), :]
    total_ref[...] += jnp.dot(weight_ref[0], rows, preferred_element_type=jnp.float32)

    @pl.when(step == pl.num_programs(0) - 1)
    def _():
        out_ref[...] = total_ref[...].astype(jnp.bfloat16)


def layer_back(where, carried, all_weights):
    pieces = tensor_pieces(carried)
    rows_local, model_width = all_weights.shape[1:]
    whole = lambda shape: pl.BlockSpec(shape, lambda i, s: (0,) * len(shape))
    return pl.pallas_call(
        layer_kernel,
        grid_spec=pltpu.PrefetchScalarGridSpec(
            num_scalar_prefetch=1,
            grid=(2,),
            in_specs=[whole(p.shape) for p in pieces]
            + [
                whole(carried.shape),
                pl.BlockSpec((1, rows_local, model_width // 2), lambda i, s: (s[5], 0, i)),
            ],
            out_specs=whole(carried.shape),
            scratch_shapes=[
                pltpu.VMEM((model_width, carried.shape[1]), jnp.bfloat16),
                pltpu.VMEM(carried.shape, jnp.float32),
            ],
        ),
        out_shape=jax.ShapeDtypeStruct(carried.shape, jnp.bfloat16),
        compiler_params=pltpu.CompilerParams(vmem_limit_bytes=wide_vmem),
    )(where, *pieces, carried, all_weights)


def weights_kernel(totals_ref, row_new_ref, col_ref, gradient_ref, weight_ref, out_ref, col_new_ref, rows_ref, cols_ref):
    step = pl.program_id(0)
    tile = weight_ref.shape[1]
    width = col_ref.shape[1]

    @pl.when(step == 0)
    def _():
        entries = float(width) * float(width)
        col_new = decay_rate * col_ref[...] + (1.0 - decay_rate) * (totals_ref[0:1, :width] / width)
        col_new_ref[...] = col_new
        cols_ref[...] = 1.0 / jnp.sqrt(col_new)
        row_total = totals_ref[0:1, width : width + 1]
        weight_total = totals_ref[1:2, width : width + 1]
        update_total = row_total * jnp.sum(totals_ref[1:2, :width] / col_new, axis=1, keepdims=True)
        factor = learn_rate * jnp.sqrt(weight_total / entries)
        factor = factor / jnp.maximum(1.0, jnp.sqrt(update_total / entries))
        rows_ref[...] = jnp.broadcast_to(factor * jnp.sqrt(row_total / row_new_ref[...]), rows_ref.shape)

    for at in range(0, tile, 128):
        here = pl.ds(pl.multiple_of(step * tile + at, 128), 128)
        change = gradient_ref[:, at : at + 128] * rows_ref[...] * cols_ref[:, here]
        weight = weight_ref[:, at : at + 128].astype(jnp.float32)
        out_ref[:, at : at + 128] = (weight - change).astype(jnp.bfloat16)


def updated_weights(totals, row_new, col_state, gradient, weight, tile=1664):
    rows, width = weight.shape
    whole = lambda shape: pl.BlockSpec(shape, lambda i: (0,) * len(shape))
    block = pl.BlockSpec((rows, tile), lambda i: (0, i))
    return pl.pallas_call(
        weights_kernel,
        grid=(width // tile,),
        in_specs=[whole(totals.shape), whole(row_new.shape), whole(col_state.shape), block, block],
        out_specs=[block, whole(col_state.shape)],
        out_shape=[
            jax.ShapeDtypeStruct((rows, width), jnp.bfloat16),
            jax.ShapeDtypeStruct(col_state.shape, jnp.float32),
        ],
        scratch_shapes=[pltpu.VMEM((rows, 128), jnp.float32), pltpu.VMEM((1, width), jnp.float32)],
        compiler_params=pltpu.CompilerParams(vmem_limit_bytes=wide_vmem),
    )(totals, row_new, col_state, gradient, weight)


def body(hidden_last, labels, head_weight, layer_inputs, weights, row_state, col_state):
    section_count = lax.axis_size("x")
    section_index = lax.axis_index("x")
    all_rows = labels.shape[0]
    model_width, vocab_local = head_weight.shape
    local_weight = weights[0]
    rows_local = local_weight.shape[0]
    saved_all = layer_inputs[0]
    share = all_rows // section_count
    row_start = section_index * share
    tensor_index = lax.axis_index(("y", "z", "c"))

    def where(layer):
        return jnp.stack(
            [
                lax.axis_index("y"),
                lax.axis_index("z"),
                lax.axis_index("c"),
                tensor_index * vocab_local,
                jnp.int32(all_rows),
                jnp.asarray(layer, jnp.int32),
            ]
        )

    all_weights = lax.all_gather(local_weight, "x", axis=0)
    hidden_rows = lax.dynamic_slice_in_dim(hidden_last, row_start, share, 0).T
    labels_here = lax.dynamic_slice_in_dim(labels, row_start, share, 0)
    hidden_all = in_order(where(0), tensor_pieces(hidden_rows))
    logits = lax.dot_general(
        head_weight, hidden_all, (((0,), (0,)), ((), ())), preferred_element_type=jnp.float32
    )
    exponent = jnp.exp(logits)
    columns = tensor_index * vocab_local + lax.iota(jnp.int32, vocab_local)
    label_hit = labels_here[None, :] == columns[:, None]
    sums = jnp.stack(
        [
            jnp.sum(exponent, axis=0),
            jnp.sum(jnp.where(label_hit, logits, jnp.zeros_like(logits)), axis=0),
        ]
    )
    sums = summed_tensor(sums)
    both = jnp.concatenate(
        [jnp.minimum(exponent, bf16_largest).astype(jnp.bfloat16), label_hit.astype(jnp.bfloat16)], axis=1
    )
    product = lax.dot_general(
        both, head_weight, (((0,), (1,)), ((), ())), preferred_element_type=jnp.float32
    )
    keep, send = head_combine(where(0), product, sums, rows_local)
    part = (keep + other_core(send).astype(jnp.float32)).astype(jnp.bfloat16)
    part = swapped_chips(part.reshape(-1, rows_local, share)).astype(jnp.float32).sum(axis=0)
    carried = part.astype(jnp.bfloat16)

    chain = [carried]
    for layer in reversed(range(1, section_count)):
        carried = layer_back(where(layer), carried, all_weights)
        chain.insert(0, carried)

    dy = exchanged(chain, "x").reshape(rows_local, all_rows)
    full = lax.all_gather(dy, ("y", "z", "c"), axis=0, tiled=True)
    loss = jnp.sum(jnp.log(sums[0]) - sums[1])[None]
    for distance in (1, 2):
        loss = loss + lax.ppermute(loss, "x", [(i, i ^ distance) for i in range(section_count)])
    loss = loss[0] / all_rows
    weight_float = local_weight.astype(jnp.float32)
    weight_part = jnp.sum(weight_float * weight_float)
    full, loss, weight_part = lax.optimization_barrier((full, loss, weight_part))
    gradient = lax.dot_general(
        saved_all, full, (((0,), (1,)), ((), ())), preferred_element_type=jnp.float32
    )
    squares = gradient * gradient
    row_new = decay_rate * row_state[0] + (1.0 - decay_rate) * jnp.mean(squares + tiny_term, axis=1)
    col_part = jnp.sum(squares + tiny_term, axis=0)
    scaled_part = jnp.sum(squares * (1.0 / row_new)[:, None], axis=0)
    room = [(0, 128, 0)]
    totals = jnp.stack([lax.pad(col_part, jnp.sum(row_new), room), lax.pad(scaled_part, weight_part, room)])
    totals = totals + other_core(totals)
    totals = summed_ring(summed_ring(totals, "z"), "y")
    row_new = row_new[:, None]
    backward = jnp.dot(local_weight, full, preferred_element_type=jnp.float32)
    outputs = (dy.astype(jnp.float32) + backward).astype(jnp.bfloat16)
    new_weight, col_new = updated_weights(totals, row_new, col_state, gradient, local_weight)
    return (loss, outputs.T[None], new_weight[None], row_new.T, col_new)


def solution(mesh):
    fine = Mesh(mesh.devices.reshape(4, 4, 4, 2), ("x", "y", "z", "c"))
    tensor = ("y", "z", "c")
    return jax.shard_map(
        body,
        mesh=fine,
        in_specs=(
            P(None, tensor),
            P(),
            P(None, tensor),
            P("x", None, tensor),
            P("x", tensor, None),
            P("x", tensor),
            P("x", None),
        ),
        out_specs=(
            P(),
            P("x", None, tensor),
            P("x", tensor, None),
            P("x", tensor),
            P("x", None),
        ),
        check_vma=False,
    )
```

```python
import jax
import jax.numpy as jnp
from jax import lax
from jax.experimental import pallas as pl
from jax.experimental.pallas import tpu as pltpu
from jax.sharding import Mesh, PartitionSpec as P

decay_rate = 0.9
learn_rate = 0.3
tiny_term = 1e-30
bf16_largest = 3.3895e38
chips = ("y", "z")
wide_vmem = 48 * 1024 * 1024


def rotated(pieces, index, axis=0):
    count = len(pieces)
    placed = []
    for k in range(count):
        chosen = pieces[k]
        for shift in range(1, count):
            chosen = jnp.where(index == shift, pieces[(k - shift) % count], chosen)
        placed.append(chosen)
    return jnp.stack(placed, axis=axis)


def other_core(x):
    return lax.ppermute(x, "c", [(0, 1), (1, 0)])


def swapped_chips(blocks):
    return lax.all_to_all(blocks, chips, 0, 0, tiled=True)


def from_chips(block):
    count = lax.axis_size(chips)
    return swapped_chips(jnp.broadcast_to(block[None], (count, *block.shape)))


def tensor_pieces(block):
    mine = from_chips(block)
    return [mine, other_core(mine)]


def summed_tensor(x):
    return jnp.sum(from_chips(x + other_core(x)), axis=0)


def summed_ring(x, axis):
    one, two, three = (
        lax.ppermute(x, axis, [(i, (i - step) % 4) for i in range(4)]) for step in (1, 2, 3)
    )
    return (x + two) + (one + three)


def exchanged(blocks, axis):
    size = lax.axis_size(axis)
    index = lax.axis_index(axis)
    pieces = []
    for step in range(size):
        piece = blocks[step]
        for shift in range(1, size):
            piece = jnp.where(index == shift, blocks[(step + shift) % size], piece)
        if step:
            piece = lax.ppermute(piece, axis, [(i, (i + step) % size) for i in range(size)])
        pieces.append(piece)
    return rotated([pieces[-k % size] for k in range(size)], index, 1)


def place(pieces, place_ref, full_ref):
    c = place_ref[2]
    count, rows = pieces[0].shape[:2]
    for chip in range(count):
        for side in range(2):
            core = c if side == 0 else 1 - c
            start = pl.multiple_of((chip * 2 + core) * rows, 16)
            full_ref[pl.ds(start, rows), :] = pieces[side][chip]


def order_kernel(place_ref, *refs):
    place(refs[:2], place_ref, refs[2])


def in_order(where, pieces):
    count, rows, tokens = pieces[0].shape
    whole = lambda shape: pl.BlockSpec(shape, lambda i, s: (0,) * len(shape))
    return pl.pallas_call(
        order_kernel,
        grid_spec=pltpu.PrefetchScalarGridSpec(
            num_scalar_prefetch=1,
            grid=(1,),
            in_specs=[whole(p.shape) for p in pieces],
            out_specs=whole((2 * count * rows, tokens)),
        ),
        out_shape=jax.ShapeDtypeStruct((2 * count * rows, tokens), jnp.bfloat16),
        compiler_params=pltpu.CompilerParams(vmem_limit_bytes=wide_vmem),
    )(where, *pieces)


def combine_kernel(place_ref, product_ref, sums_ref, keep_ref, send_ref, turned_ref):
    share = sums_ref.shape[1]
    rows = keep_ref.shape[2]
    c = place_ref[2]
    scale = (1.0 / place_ref[4].astype(jnp.float32)) / sums_ref[0:1, :]
    scale = jnp.broadcast_to(scale, (share, share)).T
    unit = 1.0 / place_ref[4].astype(jnp.float32)
    for at in range(0, product_ref.shape[1], share):
        block = product_ref[:share, at : at + share] * scale - product_ref[share:, at : at + share] * unit
        turned_ref[at : at + share, :] = block.T
    for step in range(4):
        chip = step * 2
        keep_ref[0, step] = turned_ref[pl.ds(pl.multiple_of((chip + c) * rows, 16), rows), :]
        send_ref[0, step] = turned_ref[pl.ds(pl.multiple_of((chip + 1 - c) * rows, 16), rows), :].astype(jnp.bfloat16)


def head_combine(where, product, sums, rows_local):
    width, model_width = product.shape
    share = sums.shape[1]
    tile = model_width // 4
    out_spec = pl.BlockSpec((1, 4, rows_local, share), lambda i, s: (i, 0, 0, 0))
    return pl.pallas_call(
        combine_kernel,
        grid_spec=pltpu.PrefetchScalarGridSpec(
            num_scalar_prefetch=1,
            grid=(4,),
            in_specs=[
                pl.BlockSpec((width, tile), lambda i, s: (0, i)),
                pl.BlockSpec(sums.shape, lambda i, s: (0, 0)),
            ],
            out_specs=[out_spec, out_spec],
            scratch_shapes=[pltpu.VMEM((tile, share), jnp.float32)],
        ),
        out_shape=[
            jax.ShapeDtypeStruct((4, 4, rows_local, share), jnp.float32),
            jax.ShapeDtypeStruct((4, 4, rows_local, share), jnp.bfloat16),
        ],
        compiler_params=pltpu.CompilerParams(vmem_limit_bytes=wide_vmem),
    )(where, product, sums)


def layer_kernel(place_ref, *refs):
    pieces, (carried_ref, weight_ref, out_ref, full_ref, total_ref) = refs[:2], refs[2:]
    step = pl.program_id(0)
    depth = weight_ref.shape[2]

    @pl.when(step == 0)
    def _():
        place(pieces, place_ref, full_ref)
        total_ref[...] = carried_ref[...].astype(jnp.float32)

    rows = full_ref[pl.ds(pl.multiple_of(step * depth, depth), depth), :]
    total_ref[...] += jnp.dot(weight_ref[0], rows, preferred_element_type=jnp.float32)

    @pl.when(step == pl.num_programs(0) - 1)
    def _():
        out_ref[...] = total_ref[...].astype(jnp.bfloat16)


def layer_back(where, carried, all_weights):
    pieces = tensor_pieces(carried)
    rows_local, model_width = all_weights.shape[1:]
    whole = lambda shape: pl.BlockSpec(shape, lambda i, s: (0,) * len(shape))
    return pl.pallas_call(
        layer_kernel,
        grid_spec=pltpu.PrefetchScalarGridSpec(
            num_scalar_prefetch=1,
            grid=(2,),
            in_specs=[whole(p.shape) for p in pieces]
            + [
                whole(carried.shape),
                pl.BlockSpec((1, rows_local, model_width // 2), lambda i, s: (s[5], 0, i)),
            ],
            out_specs=whole(carried.shape),
            scratch_shapes=[
                pltpu.VMEM((model_width, carried.shape[1]), jnp.bfloat16),
                pltpu.VMEM(carried.shape, jnp.float32),
            ],
        ),
        out_shape=jax.ShapeDtypeStruct(carried.shape, jnp.bfloat16),
        compiler_params=pltpu.CompilerParams(vmem_limit_bytes=wide_vmem),
    )(where, *pieces, carried, all_weights)


def weights_kernel(totals_ref, sums_ref, row_new_ref, col_ref, gradient_ref, weight_ref, out_ref, col_new_ref, rows_ref, cols_ref):
    step = pl.program_id(0)
    tile = weight_ref.shape[1]
    width = col_ref.shape[1]

    @pl.when(step == 0)
    def _():
        entries = float(width) * float(width)
        col_new = decay_rate * col_ref[...] + (1.0 - decay_rate) * (totals_ref[0:1, :width] / width)
        col_new_ref[...] = col_new
        cols_ref[...] = 1.0 / jnp.sqrt(col_new)
        squares_total = jnp.sum(totals_ref[0:1, :], axis=1, keepdims=True)
        row_total = decay_rate * sums_ref[3:4, 0:1] + (1.0 - decay_rate) * (squares_total / width)
        weight_total = sums_ref[2:3, 0:1]
        update_total = row_total * jnp.sum(totals_ref[1:2, :width] / col_new, axis=1, keepdims=True)
        factor = learn_rate * jnp.sqrt(weight_total / entries)
        factor = factor / jnp.maximum(1.0, jnp.sqrt(update_total / entries))
        rows_ref[...] = jnp.broadcast_to(factor * jnp.sqrt(row_total / row_new_ref[...]), rows_ref.shape)

    for at in range(0, tile, 128):
        here = pl.ds(pl.multiple_of(step * tile + at, 128), 128)
        change = gradient_ref[:, at : at + 128] * rows_ref[...] * cols_ref[:, here]
        weight = weight_ref[:, at : at + 128].astype(jnp.float32)
        out_ref[:, at : at + 128] = (weight - change).astype(jnp.bfloat16)


def updated_weights(totals, sums, row_new, col_state, gradient, weight, tile=1664):
    rows, width = weight.shape
    whole = lambda shape: pl.BlockSpec(shape, lambda i: (0,) * len(shape))
    block = pl.BlockSpec((rows, tile), lambda i: (0, i))
    return pl.pallas_call(
        weights_kernel,
        grid=(width // tile,),
        in_specs=[whole(totals.shape), whole(sums.shape), whole(row_new.shape), whole(col_state.shape), block, block],
        out_specs=[block, whole(col_state.shape)],
        out_shape=[
            jax.ShapeDtypeStruct((rows, width), jnp.bfloat16),
            jax.ShapeDtypeStruct(col_state.shape, jnp.float32),
        ],
        scratch_shapes=[pltpu.VMEM((rows, 128), jnp.float32), pltpu.VMEM((1, width), jnp.float32)],
        compiler_params=pltpu.CompilerParams(vmem_limit_bytes=wide_vmem),
    )(totals, sums, row_new, col_state, gradient, weight)


def body(hidden_last, labels, head_weight, layer_inputs, weights, row_state, col_state):
    section_count = lax.axis_size("x")
    section_index = lax.axis_index("x")
    all_rows = labels.shape[0]
    model_width, vocab_local = head_weight.shape
    local_weight = weights[0]
    rows_local = local_weight.shape[0]
    saved_all = layer_inputs[0]
    share = all_rows // section_count
    row_start = section_index * share
    tensor_index = lax.axis_index(("y", "z", "c"))

    def where(layer):
        return jnp.stack(
            [
                lax.axis_index("y"),
                lax.axis_index("z"),
                lax.axis_index("c"),
                tensor_index * vocab_local,
                jnp.int32(all_rows),
                jnp.asarray(layer, jnp.int32),
            ]
        )

    all_weights = lax.all_gather(local_weight, "x", axis=0)
    hidden_rows = lax.dynamic_slice_in_dim(hidden_last, row_start, share, 0).T
    labels_here = lax.dynamic_slice_in_dim(labels, row_start, share, 0)
    hidden_all = in_order(where(0), tensor_pieces(hidden_rows))
    logits = lax.dot_general(
        head_weight, hidden_all, (((0,), (0,)), ((), ())), preferred_element_type=jnp.float32
    )
    exponent = jnp.exp(logits)
    columns = tensor_index * vocab_local + lax.iota(jnp.int32, vocab_local)
    label_hit = labels_here[None, :] == columns[:, None]
    weight_float = local_weight.astype(jnp.float32)
    weight_part = jnp.broadcast_to(jnp.sum(weight_float * weight_float), (share,))
    sums = jnp.stack(
        [
            jnp.sum(exponent, axis=0),
            jnp.sum(jnp.where(label_hit, logits, jnp.zeros_like(logits)), axis=0),
            weight_part,
            jnp.broadcast_to(jnp.sum(row_state[0]), (share,)),
        ]
    )
    sums = summed_tensor(sums)
    both = jnp.concatenate(
        [jnp.minimum(exponent, bf16_largest).astype(jnp.bfloat16), label_hit.astype(jnp.bfloat16)], axis=1
    )
    product = lax.dot_general(
        both, head_weight, (((0,), (1,)), ((), ())), preferred_element_type=jnp.float32
    )
    keep, send = head_combine(where(0), product, sums, rows_local)
    part = (keep + other_core(send).astype(jnp.float32)).astype(jnp.bfloat16)
    part = swapped_chips(part.reshape(-1, rows_local, share)).astype(jnp.float32).sum(axis=0)
    carried = part.astype(jnp.bfloat16)

    chain = [carried]
    for layer in reversed(range(1, section_count)):
        carried = layer_back(where(layer), carried, all_weights)
        chain.insert(0, carried)

    dy = exchanged(chain, "x").reshape(rows_local, all_rows)
    full = lax.all_gather(dy, ("y", "z", "c"), axis=0, tiled=True)
    loss = jnp.sum(jnp.log(sums[0]) - sums[1])[None]
    for distance in (1, 2):
        loss = loss + lax.ppermute(loss, "x", [(i, i ^ distance) for i in range(section_count)])
    loss = loss[0] / all_rows
    full, loss = lax.optimization_barrier((full, loss))
    gradient = lax.dot_general(
        saved_all, full, (((0,), (1,)), ((), ())), preferred_element_type=jnp.float32
    )
    squares = gradient * gradient
    row_new = decay_rate * row_state[0] + (1.0 - decay_rate) * jnp.mean(squares + tiny_term, axis=1)
    col_part = jnp.sum(squares + tiny_term, axis=0)
    scaled_part = jnp.sum(squares * (1.0 / row_new)[:, None], axis=0)
    totals = jnp.stack([col_part, scaled_part])
    totals = totals + other_core(totals)
    totals = summed_ring(summed_ring(totals, "z"), "y")
    row_new = row_new[:, None]
    backward = jnp.dot(local_weight, full, preferred_element_type=jnp.float32)
    outputs = (dy.astype(jnp.float32) + backward).astype(jnp.bfloat16)
    new_weight, col_new = updated_weights(totals, sums, row_new, col_state, gradient, local_weight)
    return (loss, outputs.T[None], new_weight[None], row_new.T, col_new)


def solution(mesh):
    fine = Mesh(mesh.devices.reshape(4, 4, 4, 2), ("x", "y", "z", "c"))
    tensor = ("y", "z", "c")
    return jax.shard_map(
        body,
        mesh=fine,
        in_specs=(
            P(None, tensor),
            P(),
            P(None, tensor),
            P("x", None, tensor),
            P("x", tensor, None),
            P("x", tensor),
            P("x", None),
        ),
        out_specs=(
            P(),
            P("x", None, tensor),
            P("x", tensor, None),
            P("x", tensor),
            P("x", None),
        ),
        check_vma=False,
    )
```
